256 devices in a mesh: dp: 8 (over x, core), graph: 32 (over y, z).
Axes of the slice: x: 4, y: 4, z: 8, core: 2. Of those that a mesh axis runs over, the one named last changes fastest.
Arguments:
- edges: bfloat16 [8, 65536, 1024], P('dp', 'graph'), may hold values from -6 to 6
- send_rows: int32 [8, 262144], P('dp', 'graph'), may hold values from 0 to 2047
- trip_src: int32 [8, 262144], P('dp', 'graph'), may hold values from 0 to 8191
- trip_dst: int32 [8, 262144], P('dp', 'graph'), may hold values from 0 to 2047
- basis_values: bfloat16 [8, 42, 262144], P('dp', None, 'graph'), may hold values from -6 to 6
- cotangent: bfloat16 [8, 65536, 1024], P('dp', 'graph'), may hold values from -6 to 6
- w_down: bfloat16 [1024, 128], replicated, may hold values from -0.1875 to 0.1875
- w_up: bfloat16 [128, 1024], replicated, may hold values from -0.5 to 0.5
- w_basis: bfloat16 [42, 128], replicated, may hold values from -1 to 1
Outputs:
- grad_edges: bfloat16 [8, 65536, 1024], P('dp', 'graph')
- grad_down: float32 [1024, 128], replicated
- grad_up: float32 [128, 1024], replicated
- grad_basis: float32 [42, 128], replicated
The draws below stay inside these ranges and needn't reach their ends.
All inputs are finite; a program needn't handle non-finite values.
Results may differ from the reference program's by a relative error of at most 0.0073.
Values may be sent and summed in bfloat16 or wider, within the bound.
No kernel may reach another device: no remote copies, remote signals or barrier semaphores. Data moves between devices by JAX's collectives and lax.ppermute only.
A program may use at most 128 MiB of HBM per device.

```python
import jax
import jax.numpy as jnp
from jax import lax

D = 1024
TW = 128
NB = 42
E_DEV = 2048
TRIP_DEV = 8192
RECV_DEV = 8192
SLOT = 256
EDGES = 65536
TRIPS = 262144
N_DP = 8
N_GRAPH = 32


def touch_ends(values, stream_key, smallest, top_value):
    longest = values.shape.index(max(values.shape))
    spots = []
    for shift in (0, 1):
        where = [jax.random.randint(jax.random.fold_in(stream_key, axis), (), 0, length) for axis, length in enumerate(values.shape)]
        where[longest] = (where[longest] + shift) % values.shape[longest]
        spots.append(tuple(where))
    return values.at[spots[0]].set(smallest).at[spots[1]].set(top_value)


def shard_levels(key, shape, pieces, smallest, high):
    loudness, own = 1.0, jax.random.fold_in(key, 6)
    for axis_at, blocks in pieces:
        draws = jnp.exp(jax.random.uniform(jax.random.fold_in(own, axis_at), (blocks,), jnp.float32, smallest / len(pieces), high / len(pieces)))
        loudness = loudness * jnp.repeat(draws, shape[axis_at] // blocks).reshape([-1 if axis == axis_at else 1 for axis in range(len(shape))])
    return loudness


def normal_values(own_key, dims, scale, reach, split=(), held_as=jnp.bfloat16):
    gain = shard_levels(own_key, dims, split, -0.22, 0.18) if split else 1.0
    result = jax.random.normal(own_key, dims, jnp.float32) * scale * gain
    return jnp.minimum(jnp.maximum(result, -reach), reach).astype(held_as)


def setup_inputs(seed: int = 0) -> dict:
    key_list = jax.random.split(jax.random.key(seed), 10)
    edges = normal_values(key_list[0], (N_DP, EDGES, D), 1.0, 6.0, ((0, 8), (1, 32)))
    send_rows = touch_ends(jax.random.randint(key_list[1], (N_DP, N_GRAPH * RECV_DEV), 0, E_DEV), jax.random.fold_in(key_list[1], 1), 0, E_DEV - 1).astype(jnp.int32)
    trip_src = touch_ends(jax.random.randint(key_list[2], (N_DP, TRIPS), 0, RECV_DEV), jax.random.fold_in(key_list[2], 1), 0, RECV_DEV - 1).astype(jnp.int32)
    trip_dst = touch_ends(jax.random.randint(key_list[3], (N_DP, TRIPS), 0, E_DEV), jax.random.fold_in(key_list[3], 1), 0, E_DEV - 1).astype(jnp.int32)
    basis_values = normal_values(key_list[4], (N_DP, NB, TRIPS), 1.0, 6.0, ((0, 8), (2, 32)))
    cotangent = normal_values(key_list[5], (N_DP, EDGES, D), 1.0, 6.0, ((0, 8), (1, 32)))
    w_down = normal_values(key_list[6], (D, TW), D ** -0.5, 0.1875)
    w_up = normal_values(key_list[7], (TW, D), TW ** -0.5, 0.5)
    w_basis = normal_values(key_list[8], (NB, TW), NB ** -0.5, 1.0)
    return dict(edges=edges, send_rows=send_rows, trip_src=trip_src, trip_dst=trip_dst, basis_values=basis_values, cotangent=cotangent, w_down=w_down, w_up=w_up, w_basis=w_basis)


def device_work(received_rows, source_index, target_index, basis_block, grad_block, w_up, w_basis):
    source_rows = received_rows[source_index].astype(jnp.float32)
    basis_emb = jnp.dot(basis_block.T, w_basis, preferred_element_type=jnp.float32)
    product = source_rows * basis_emb
    aggregate = jax.ops.segment_sum(product, target_index, num_segments=E_DEV).astype(jnp.bfloat16)
    pre_act = jnp.dot(aggregate, w_up, preferred_element_type=jnp.float32)
    sigma = jax.nn.sigmoid(pre_act)
    g_pre = (grad_block.astype(jnp.float32) * sigma * (1.0 + pre_act * (1.0 - sigma))).astype(jnp.bfloat16)
    up_term = jnp.dot(aggregate.T, g_pre, preferred_element_type=jnp.float32)
    g_agg = jnp.dot(g_pre, w_up.T, preferred_element_type=jnp.float32)
    g_trip = g_agg[target_index]
    g_source = g_trip * basis_emb
    g_basis_emb = g_trip * source_rows
    basis_term = jnp.dot(basis_block.astype(jnp.float32), g_basis_emb, precision=lax.Precision.HIGHEST)
    g_received = jax.ops.segment_sum(g_source, source_index, num_segments=RECV_DEV)
    return g_received, up_term, basis_term


def one_batch(edges, send_rows, trip_src, trip_dst, basis_values, cotangent, w_down, w_up, w_basis):
    devices = N_GRAPH
    down = jnp.dot(edges, w_down, preferred_element_type=jnp.float32).astype(jnp.bfloat16)
    table = send_rows.reshape(devices, devices, SLOT)
    offsets = jnp.arange(devices, dtype=jnp.int32) * E_DEV
    picks = (jnp.transpose(table, (1, 0, 2)) + offsets[None, :, None]).astype(jnp.int32)
    received = down[picks.reshape(devices, RECV_DEV)]
    sources = trip_src.reshape(devices, TRIP_DEV)
    targets = trip_dst.reshape(devices, TRIP_DEV)
    basis_blocks = jnp.transpose(basis_values.reshape(NB, devices, TRIP_DEV), (1, 0, 2))
    grad_blocks = cotangent.reshape(devices, E_DEV, D)
    g_received, up_terms, basis_terms = jax.vmap(device_work, in_axes=(0, 0, 0, 0, 0, None, None))(
        received, sources, targets, basis_blocks, grad_blocks, w_up, w_basis)
    g_down = jax.ops.segment_sum(g_received.reshape(devices * RECV_DEV, TW), picks.reshape(-1),
                                 num_segments=EDGES).astype(jnp.bfloat16)
    grad_edges = jnp.dot(g_down, w_down.T, preferred_element_type=jnp.float32).astype(jnp.bfloat16)
    down_term = lax.dot_general(edges, g_down, (((0,), (0,)), ((), ())), preferred_element_type=jnp.float32)
    return grad_edges, down_term, jnp.sum(up_terms, axis=0), jnp.sum(basis_terms, axis=0)


def reference(edges, send_rows, trip_src, trip_dst, basis_values, cotangent, w_down, w_up, w_basis):
    def run_batch(batch_args):
        return one_batch(*batch_args, w_down, w_up, w_basis)

    grad_edges, down_terms, up_terms, basis_terms = lax.map(
        run_batch, (edges, send_rows, trip_src, trip_dst, basis_values, cotangent))
    return grad_edges, jnp.sum(down_terms, axis=0), jnp.sum(up_terms, axis=0), jnp.sum(basis_terms, axis=0)
```

```python
import jax
import jax.numpy as jnp
from jax import lax
from jax.experimental import pallas as pl
from jax.experimental.pallas import tpu as pltpu
from jax.sharding import PartitionSpec as P

LO = 256
BF = jnp.bfloat16
F32 = jnp.float32


def split(idx):
    return idx & (LO - 1), idx >> 8


def onehot(lo, width):
    rows = lax.broadcasted_iota(jnp.int32, (LO, width), 0)
    return jnp.where(rows == lo, 1.0, 0.0).astype(BF)


def nn(a, b):
    return jnp.dot(a, b, preferred_element_type=F32)


def nt(a, b):
    return lax.dot_general(a, b, (((1,), (1,)), ((), ())), preferred_element_type=F32)


def tn(a, b):
    return lax.dot_general(a, b, (((0,), (0,)), ((), ())), preferred_element_type=F32)


def pick(res, hi, blocks, feats, base=0):
    acc = jnp.zeros((feats, res.shape[1]), F32)
    for j in range(blocks):
        acc = jnp.where(hi == base + j, res[j * feats:(j + 1) * feats], acc)
    return acc


def params():
    return pltpu.CompilerParams(vmem_limit_bytes=56 * 1024 * 1024)


def full(shape):
    return pl.BlockSpec(shape, lambda i: (0,) * len(shape))


def send_kernel(edges, w_down, send_idx, peers):
    n_edges, width = edges.shape
    feats = w_down.shape[1]
    eb = 512
    nd = n_edges // eb
    per = 4
    ng = peers // per
    slot = send_idx.shape[1] // peers
    blocks = n_edges // LO

    def body(e_ref, w_ref, i_ref, out_ref, table):
        i = pl.program_id(0)

        @pl.when(i < nd)
        def _():
            d = nn(e_ref[...], w_ref[...]).astype(BF).T
            for k in range(eb // LO):
                table[i * (eb // LO) + k] = d[:, k * LO:(k + 1) * LO]

        @pl.when(i >= nd)
        def _():
            tab = table[...].reshape(blocks * feats, LO)
            for a in range(per):
                lo, hi = split(i_ref[:, a * slot:(a + 1) * slot])
                res = nn(tab, onehot(lo, slot))
                out_ref[a] = pick(res, hi, blocks, feats).astype(BF)

    return pl.pallas_call(
        body,
        out_shape=jax.ShapeDtypeStruct((peers, feats, slot), BF),
        grid=(nd + ng,),
        in_specs=[
            pl.BlockSpec((eb, width), lambda i: (jnp.minimum(i, nd - 1), 0)),
            full(w_down.shape),
            pl.BlockSpec((1, per * slot), lambda i: (0, jnp.maximum(i - nd, 0))),
        ],
        out_specs=pl.BlockSpec((per, feats, slot), lambda i: (jnp.maximum(i - nd, 0), 0, 0)),
        scratch_shapes=[pltpu.VMEM((blocks, feats, LO), BF)],
        compiler_params=params(),
        name="send",
    )(edges, w_down, send_idx)


def forward_kernel(recv, src, dst, basis, w_basis_t, n_edges):
    peers, feats, _ = recv.shape
    trips = src.shape[1]
    nb = basis.shape[0]
    tc = 1024
    steps = trips // tc
    eblocks = n_edges // LO

    def body(r_ref, s_ref, d_ref, b_ref, w_ref, src_out, agg_out, acc, pm, oh):
        i = pl.program_id(0)

        @pl.when(i == 0)
        def _():
            acc[...] = jnp.zeros_like(acc)

        tab = r_ref[...].reshape(peers * feats, LO)
        for a in range(tc // LO):
            cols = slice(a * LO, (a + 1) * LO)
            lo, hi = split(s_ref[:, cols])
            source = pick(nn(tab, onehot(lo, LO)), hi, peers, feats)
            src_out[:, cols] = source.astype(BF)
            product = source * nn(w_ref[...], b_ref[:, cols])
            lo, hi = split(d_ref[:, cols])
            for j in range(eblocks):
                pm[j * feats:(j + 1) * feats, cols] = jnp.where(hi == j, product, 0.0).astype(BF)
            oh[:, cols] = onehot(lo, LO)
        acc[...] += nt(pm[...], oh[...])

        @pl.when(i == steps - 1)
        def _():
            for j in range(eblocks):
                agg_out[:, j * LO:(j + 1) * LO] = acc[j * feats:(j + 1) * feats].astype(BF)

    return pl.pallas_call(
        body,
        out_shape=(
            jax.ShapeDtypeStruct((feats, trips), BF),
            jax.ShapeDtypeStruct((feats, n_edges), BF),
        ),
        grid=(steps,),
        in_specs=[
            full(recv.shape),
            pl.BlockSpec((1, tc), lambda i: (0, i)),
            pl.BlockSpec((1, tc), lambda i: (0, i)),
            pl.BlockSpec((nb, tc), lambda i: (0, i)),
            full(w_basis_t.shape),
        ],
        out_specs=(pl.BlockSpec((feats, tc), lambda i: (0, i)), full((feats, n_edges))),
        scratch_shapes=[
            pltpu.VMEM((eblocks * feats, LO), F32),
            pltpu.VMEM((eblocks * feats, tc), BF),
            pltpu.VMEM((LO, tc), BF),
        ],
        compiler_params=params(),
        name="forward",
    )(recv, src, dst, basis, w_basis_t)


def dense_kernel(agg_t, w_up, cot):
    feats, n_edges = agg_t.shape
    width = w_up.shape[1]
    eb = 256
    steps = n_edges // eb

    def body(a_ref, w_ref, c_ref, up_out, g_out):
        i = pl.program_id(0)
        agg = a_ref[...]
        pre = tn(agg, w_ref[...])
        sig = 1.0 / (1.0 + jnp.exp(-pre))
        g_pre = (c_ref[...].astype(F32) * sig * (1.0 + pre * (1.0 - sig))).astype(BF)

        @pl.when(i == 0)
        def _():
            up_out[...] = jnp.zeros_like(up_out)

        up_out[...] += nn(agg, g_pre)
        g_out[...] = nt(w_ref[...], g_pre).astype(BF)

    return pl.pallas_call(
        body,
        out_shape=(
            jax.ShapeDtypeStruct((feats, width), F32),
            jax.ShapeDtypeStruct((feats, n_edges), BF),
        ),
        grid=(steps,),
        in_specs=[
            pl.BlockSpec((feats, eb), lambda i: (0, i)),
            full(w_up.shape),
            pl.BlockSpec((eb, width), lambda i: (i, 0)),
        ],
        out_specs=(full((feats, width)), pl.BlockSpec((feats, eb), lambda i: (0, i))),
        compiler_params=params(),
        name="dense",
    )(agg_t, w_up, cot)


def backward_kernel(g_agg_t, src_t, src, dst, basis, w_basis_t, peers):
    feats, n_edges = g_agg_t.shape
    trips = src.shape[1]
    nb = basis.shape[0]
    tc = 1024
    steps = trips // tc
    eblocks = n_edges // LO

    def body(g_ref, st_ref, s_ref, d_ref, b_ref, w_ref, out_ref, bt_out, table, acc, pm, oh):
        i = pl.program_id(0)

        @pl.when(i == 0)
        def _():
            acc[...] = jnp.zeros_like(acc)
            bt_out[...] = jnp.zeros_like(bt_out)
            for j in range(eblocks):
                table[j * feats:(j + 1) * feats] = g_ref[:, j * LO:(j + 1) * LO]

        for a in range(tc // LO):
            cols = slice(a * LO, (a + 1) * LO)
            lo, hi = split(d_ref[:, cols])
            g_trip = pick(nn(table[...], onehot(lo, LO)), hi, eblocks, feats)
            g_source = g_trip * nn(w_ref[...], b_ref[:, cols])
            g_basis = g_trip * st_ref[:, cols].astype(F32)
            top = g_basis.astype(BF)
            low = (g_basis - top.astype(F32)).astype(BF)
            bt_out[...] += nt(b_ref[:, cols], top) + nt(b_ref[:, cols], low)
            lo, hi = split(s_ref[:, cols])
            for j in range(peers):
                pm[j * feats:(j + 1) * feats, cols] = jnp.where(hi == j, g_source, 0.0).astype(BF)
            oh[:, cols] = onehot(lo, LO)
        acc[...] += nt(pm[...], oh[...])

        @pl.when(i == steps - 1)
        def _():
            out_ref[...] = acc[...].astype(BF).reshape(out_ref.shape)

    return pl.pallas_call(
        body,
        out_shape=(
            jax.ShapeDtypeStruct((peers, feats, LO), BF),
            jax.ShapeDtypeStruct((nb, feats), F32),
        ),
        grid=(steps,),
        in_specs=[
            full(g_agg_t.shape),
            pl.BlockSpec((feats, tc), lambda i: (0, i)),
            pl.BlockSpec((1, tc), lambda i: (0, i)),
            pl.BlockSpec((1, tc), lambda i: (0, i)),
            pl.BlockSpec((nb, tc), lambda i: (0, i)),
            full(w_basis_t.shape),
        ],
        out_specs=(full((peers, feats, LO)), full((nb, feats))),
        scratch_shapes=[
            pltpu.VMEM((eblocks * feats, LO), BF),
            pltpu.VMEM((peers * feats, LO), F32),
            pltpu.VMEM((peers * feats, tc), BF),
            pltpu.VMEM((LO, tc), BF),
        ],
        compiler_params=params(),
        name="backward",
    )(g_agg_t, src_t, src, dst, basis, w_basis_t)


def return_kernel(ret, send_idx, edges):
    peers, feats, slot = ret.shape
    n_edges, width = edges.shape
    per = 8
    steps = peers // per
    eblocks = n_edges // LO
    eb = 512
    esteps = n_edges // eb

    def body(r_ref, i_ref, e_ref, down_out, grad_out, acc, pm, oh, gacc):
        i = pl.program_id(0)

        @pl.when(i == 0)
        def _():
            acc[...] = jnp.zeros_like(acc)
            gacc[...] = jnp.zeros_like(gacc)

        @pl.when(i < steps)
        def _():
            for a in range(per):
                cols = slice(a * slot, (a + 1) * slot)
                lo, hi = split(i_ref[:, cols])
                rows = r_ref[a].astype(F32)
                for j in range(eblocks):
                    pm[j * feats:(j + 1) * feats, cols] = jnp.where(hi == j, rows, 0.0).astype(BF)
                oh[:, cols] = onehot(lo, slot)
            acc[...] += nt(pm[...], oh[...])

        @pl.when(i == steps - 1)
        def _():
            for j in range(eblocks):
                down_out[:, j * LO:(j + 1) * LO] = acc[j * feats:(j + 1) * feats].astype(BF)

        @pl.when(i >= steps)
        def _():
            k = i - steps
            gacc[...] += nn(down_out[:, pl.ds(pl.multiple_of(k * eb, eb), eb)], e_ref[...])

        @pl.when(i == steps + esteps - 1)
        def _():
            grad_out[...] = gacc[...].T.astype(BF)

    return pl.pallas_call(
        body,
        out_shape=(
            jax.ShapeDtypeStruct((feats, n_edges), BF),
            jax.ShapeDtypeStruct((width, feats), BF),
        ),
        grid=(steps + esteps,),
        in_specs=[
            pl.BlockSpec((per, feats, slot), lambda i: (jnp.minimum(i, steps - 1), 0, 0)),
            pl.BlockSpec((1, per * slot), lambda i: (0, jnp.minimum(i, steps - 1))),
            pl.BlockSpec((eb, width), lambda i: (jnp.maximum(i - steps, 0), 0)),
        ],
        out_specs=(full((feats, n_edges)), full((width, feats))),
        scratch_shapes=[
            pltpu.VMEM((eblocks * feats, LO), F32),
            pltpu.VMEM((eblocks * feats, per * slot), BF),
            pltpu.VMEM((LO, per * slot), BF),
            pltpu.VMEM((feats, width), F32),
        ],
        compiler_params=params(),
        name="returned",
    )(ret, send_idx, edges)


def edges_kernel(g_down_t, w_down_t):
    feats, n_edges = g_down_t.shape
    width = w_down_t.shape[1]
    eb = 512

    def body(g_ref, w_ref, out_ref):
        out_ref[...] = tn(g_ref[...], w_ref[...]).astype(BF)

    return pl.pallas_call(
        body,
        out_shape=jax.ShapeDtypeStruct((n_edges, width), BF),
        grid=(n_edges // eb,),
        in_specs=[pl.BlockSpec((feats, eb), lambda i: (0, i)), full(w_down_t.shape)],
        out_specs=pl.BlockSpec((eb, width), lambda i: (i, 0)),
        compiler_params=params(),
        name="grad_edges",
    )(g_down_t, w_down_t)


def exchange(x, axes):
    return lax.all_to_all(x, axes, split_axis=0, concat_axis=0, tiled=True)


def reduce_all(x, n):
    rows, feats = x.shape
    mine = exchange(x, ("dp", "graph")).reshape(n, rows // n, feats).astype(F32).sum(axis=0)
    spread = jnp.broadcast_to(mine.astype(BF)[None], (n,) + mine.shape).reshape(rows, feats)
    return exchange(spread, ("dp", "graph"))


def make_shards(n_dp, n_graph):
    n = n_dp * n_graph

    def shards(edges, send_rows, trip_src, trip_dst, basis_values, cotangent, w_down, w_up, w_basis):
        edge_rows = edges[0]
        basis = basis_values[0]
        n_edges, width = edge_rows.shape
        feats = w_down.shape[1]
        nb = basis.shape[0]
        w_basis_t = w_basis.T
        sent = send_kernel(edge_rows, w_down, send_rows, n_graph)
        received = exchange(sent, "graph")
        src_t, agg_t = forward_kernel(received, trip_src, trip_dst, basis, w_basis_t, n_edges)
        up_term, g_agg_t = dense_kernel(agg_t, w_up, cotangent[0])
        g_received, basis_term = backward_kernel(
            g_agg_t, src_t, trip_src, trip_dst, basis, w_basis_t, n_graph
        )
        returned = exchange(g_received, "graph")
        pad = -nb % n
        small = jnp.concatenate(
            [up_term.reshape(width, feats), basis_term, jnp.zeros((pad, feats), F32)]
        ).astype(BF)
        reduced = reduce_all(small, n).astype(F32)
        g_down_t, down_term = return_kernel(returned, send_rows, edge_rows)
        grad_down = reduce_all(down_term, n).astype(F32)
        grad_edges = edges_kernel(g_down_t, w_down.T)
        grad_up = reduced[:width].reshape(feats, width)
        grad_basis = reduced[width:width + nb]
        return grad_edges[None], grad_down, grad_up, grad_basis

    return shards


def solution(mesh):
    shape = dict(mesh.shape)
    in_specs = (
        P("dp", "graph", None),
        P("dp", "graph"),
        P("dp", "graph"),
        P("dp", "graph"),
        P("dp", None, "graph"),
        P("dp", "graph", None),
        P(),
        P(),
        P(),
    )
    out_specs = (P("dp", "graph", None), P(), P(), P())
    return jax.shard_map(
        make_shards(shape["dp"], shape["graph"]),
        mesh=mesh,
        in_specs=in_specs,
        out_specs=out_specs,
        check_vma=False,
    )
```

```python
import jax
import jax.numpy as jnp
from jax import lax
from jax.experimental import pallas as pl
from jax.experimental.pallas import tpu as pltpu
from jax.sharding import PartitionSpec as P

LO = 256
BF = jnp.bfloat16
F32 = jnp.float32


def split(idx):
    return idx & (LO - 1), idx >> 8


def onehot(lo, width):
    rows = lax.broadcasted_iota(jnp.int32, (LO, width), 0)
    return jnp.where(rows == lo, 1.0, 0.0).astype(BF)


def nn(a, b):
    return jnp.dot(a, b, preferred_element_type=F32)


def nt(a, b):
    return lax.dot_general(a, b, (((1,), (1,)), ((), ())), preferred_element_type=F32)


def tn(a, b):
    return lax.dot_general(a, b, (((0,), (0,)), ((), ())), preferred_element_type=F32)


def pick(res, hi, blocks, feats, base=0):
    acc = jnp.zeros((feats, res.shape[1]), F32)
    for j in range(blocks):
        acc = jnp.where(hi == base + j, res[j * feats:(j + 1) * feats], acc)
    return acc


def params():
    return pltpu.CompilerParams(vmem_limit_bytes=56 * 1024 * 1024)


def full(shape):
    return pl.BlockSpec(shape, lambda i: (0,) * len(shape))


def send_kernel(edges, w_down, send_idx, peers):
    n_edges, width = edges.shape
    feats = w_down.shape[1]
    eb = 512
    nd = n_edges // eb
    per = 4
    ng = peers // per
    slot = send_idx.shape[1] // peers
    blocks = n_edges // LO

    def body(e_ref, w_ref, i_ref, out_ref, table):
        i = pl.program_id(0)

        @pl.when(i < nd)
        def _():
            d = nn(e_ref[...], w_ref[...]).astype(BF).T
            for k in range(eb // LO):
                table[i * (eb // LO) + k] = d[:, k * LO:(k + 1) * LO]

        @pl.when(i >= nd)
        def _():
            tab = table[...].reshape(blocks * feats, LO)
            for a in range(per):
                lo, hi = split(i_ref[:, a * slot:(a + 1) * slot])
                res = nn(tab, onehot(lo, slot))
                out_ref[a] = pick(res, hi, blocks, feats).astype(BF)

    return pl.pallas_call(
        body,
        out_shape=jax.ShapeDtypeStruct((peers, feats, slot), BF),
        grid=(nd + ng,),
        in_specs=[
            pl.BlockSpec((eb, width), lambda i: (jnp.minimum(i, nd - 1), 0)),
            full(w_down.shape),
            pl.BlockSpec((1, per * slot), lambda i: (0, jnp.maximum(i - nd, 0))),
        ],
        out_specs=pl.BlockSpec((per, feats, slot), lambda i: (jnp.maximum(i - nd, 0), 0, 0)),
        scratch_shapes=[pltpu.VMEM((blocks, feats, LO), BF)],
        compiler_params=params(),
        name="send",
    )(edges, w_down, send_idx)


def sort_kernel(src, dst, basis, peers):
    trips = src.shape[1]
    nb = basis.shape[0]
    rows = -(-(nb + 4) // 16) * 16
    chunks = trips // LO
    tc = 1024
    steps = trips // tc

    def body(s_ref, d_ref, b_ref, x_out, range_out, oh_hi, first, pm, oh, acc):
        i = pl.program_id(0)

        @pl.when(i == 0)
        def _():
            acc[...] = jnp.zeros_like(acc)
            bucket = lax.broadcasted_iota(jnp.int32, (peers, trips), 0)
            hot = jnp.where(bucket == (s_ref[...] >> 8), 1.0, 0.0)
            oh_hi[...] = hot.astype(BF)
            total = jnp.broadcast_to(jnp.sum(hot, axis=1, keepdims=True), (peers, 128))
            high = jnp.floor(total * (1.0 / 256.0))
            low = total - high * 256.0
            r = lax.broadcasted_iota(jnp.int32, (peers, peers), 0)
            c = lax.broadcasted_iota(jnp.int32, (peers, peers), 1)
            before = jnp.where(c < r, 1.0, 0.0).astype(BF)
            start = 256.0 * nn(before, high.astype(BF)) + nn(before, low.astype(BF))
            first[...] = start
            edge = 256.0 * lax.broadcasted_iota(jnp.int32, (peers, 128), 1).astype(F32)
            b0 = jnp.sum(jnp.where(start + total <= edge, 1.0, 0.0), axis=0, keepdims=True)
            b1 = jnp.sum(jnp.where(start < edge + 256.0, 1.0, 0.0), axis=0, keepdims=True) - 1.0
            range_out[0:1] = jnp.minimum(b0, peers - 1.0).astype(jnp.int32)
            range_out[1:2] = b1.astype(jnp.int32)

        r = lax.broadcasted_iota(jnp.int32, (LO, LO), 0)
        c = lax.broadcasted_iota(jnp.int32, (LO, LO), 1)
        upto = jnp.where(r <= c, 1.0, 0.0).astype(BF)
        for a in range(tc // LO):
            cols = slice(a * LO, (a + 1) * LO)
            at = pl.multiple_of(i * tc + a * LO, LO)
            hot = oh_hi[:, pl.ds(at, LO)]
            count = nn(hot, upto)
            place = first[:, 0:1] + count - 1.0
            hot32 = hot.astype(F32)
            pos = jnp.sum(hot32 * place, axis=0, keepdims=True).astype(jnp.int32)
            first[...] += jnp.broadcast_to(count[:, LO - 1:LO], first.shape)
            s_lo, s_hi = split(s_ref[:, pl.ds(at, LO)])
            d_lo, d_hi = split(d_ref[:, cols])
            row = lax.broadcasted_iota(jnp.int32, (rows - nb, LO), 0)
            extra = jnp.where(row == 0, s_lo, jnp.where(row == 1, s_hi, jnp.where(row == 2, d_lo, jnp.where(row == 3, d_hi, 0))))
            x = jnp.concatenate([b_ref[:, cols].astype(F32), extra.astype(F32)], axis=0)
            lo, hi = split(pos)
            for j in range(chunks):
                pm[j * rows:(j + 1) * rows, cols] = jnp.where(hi == j, x, 0.0).astype(BF)
            oh[:, cols] = onehot(lo, LO)
        acc[...] += nt(pm[...], oh[...])

        @pl.when(i == steps - 1)
        def _():
            x_out[...] = acc[...].reshape(x_out.shape)

    return pl.pallas_call(
        body,
        out_shape=(
            jax.ShapeDtypeStruct((chunks, rows, LO), F32),
            jax.ShapeDtypeStruct((2, 128), jnp.int32),
        ),
        grid=(steps,),
        in_specs=[
            full(src.shape),
            pl.BlockSpec((1, tc), lambda i: (0, i)),
            pl.BlockSpec((nb, tc), lambda i: (0, i)),
        ],
        out_specs=(full((chunks, rows, LO)), full((2, 128))),
        scratch_shapes=[
            pltpu.VMEM((peers, trips), BF),
            pltpu.VMEM((peers, 128), F32),
            pltpu.VMEM((chunks * rows, tc), BF),
            pltpu.VMEM((LO, tc), BF),
            pltpu.VMEM((chunks * rows, LO), F32),
        ],
        compiler_params=params(),
        name="order",
    )(src, dst, basis)


NEAR = 3


def forward_kernel(recv, ranges, trip, w_basis_t, n_edges, nb):
    peers, feats, _ = recv.shape
    chunks, rows, _ = trip.shape
    per = 8
    steps = chunks // per
    eblocks = n_edges // LO

    def body(rg, r_ref, x_ref, w_ref, src_out, agg_out, acc, pm, oh, source):
        i = pl.program_id(0)

        @pl.when(i == 0)
        def _():
            acc[...] = jnp.zeros_like(acc)

        def ids(a, k):
            return x_ref[a, nb + k:nb + k + 1].astype(jnp.int32)

        far = jnp.int32(0)
        for a in range(per):
            b0 = rg[0, i * per + a]
            far = jnp.maximum(far, rg[1, i * per + a] - b0)
            hot = onehot(ids(a, 0), LO)
            hi = ids(a, 1)
            got = jnp.zeros((feats, LO), F32)
            for n in range(NEAR):
                res = nn(r_ref[jnp.minimum(b0 + n, peers - 1)], hot)
                got = jnp.where(hi == b0 + n, res, got)
            source[a] = got

        @pl.when(far >= NEAR)
        def _():
            for a in range(per):
                def more(b, _, a=a):
                    res = nn(r_ref[b], onehot(ids(a, 0), LO))
                    source[a] = jnp.where(ids(a, 1) == b, res, source[a])
                    return 0
                lax.fori_loop(rg[0, i * per + a] + NEAR, rg[1, i * per + a] + 1, more, 0)

        for a in range(per):
            cols = slice(a * LO, (a + 1) * LO)
            src_out[a] = source[a].astype(BF)
            product = source[a] * nn(w_ref[...], x_ref[a].astype(BF))
            hi = ids(a, 3)
            for j in range(eblocks):
                pm[j * feats:(j + 1) * feats, cols] = jnp.where(hi == j, product, 0.0).astype(BF)
            oh[:, cols] = onehot(ids(a, 2), LO)
        acc[...] += nt(pm[...], oh[...])

        @pl.when(i == steps - 1)
        def _():
            for j in range(eblocks):
                agg_out[:, j * LO:(j + 1) * LO] = acc[j * feats:(j + 1) * feats].astype(BF)

    def whole(shape):
        return pl.BlockSpec(shape, lambda i, rg: (0,) * len(shape))

    return pl.pallas_call(
        body,
        out_shape=(
            jax.ShapeDtypeStruct((chunks, feats, LO), BF),
            jax.ShapeDtypeStruct((feats, n_edges), BF),
        ),
        grid_spec=pltpu.PrefetchScalarGridSpec(
            num_scalar_prefetch=1,
            grid=(steps,),
            in_specs=[
                whole(recv.shape),
                pl.BlockSpec((per, rows, LO), lambda i, rg: (i, 0, 0)),
                whole(w_basis_t.shape),
            ],
            out_specs=(
                pl.BlockSpec((per, feats, LO), lambda i, rg: (i, 0, 0)),
                whole((feats, n_edges)),
            ),
            scratch_shapes=[
                pltpu.VMEM((eblocks * feats, LO), F32),
                pltpu.VMEM((eblocks * feats, per * LO), BF),
                pltpu.VMEM((LO, per * LO), BF),
                pltpu.VMEM((per, feats, LO), F32),
            ],
        ),
        compiler_params=params(),
        name="forward",
    )(ranges, recv, trip, w_basis_t)


def dense_kernel(agg_t, w_up, cot):
    feats, n_edges = agg_t.shape
    width = w_up.shape[1]
    eb = 256
    steps = n_edges // eb

    def body(a_ref, w_ref, c_ref, p_out, g_out):
        pre = tn(a_ref[...], w_ref[...])
        t = 0.5 * jnp.tanh(0.5 * pre)
        g_pre = (c_ref[...].astype(F32) * (0.5 + t) * (1.0 + pre * (0.5 - t))).astype(BF)
        p_out[...] = g_pre
        g_out[...] = nt(w_ref[...], g_pre).astype(BF)

    return pl.pallas_call(
        body,
        out_shape=(
            jax.ShapeDtypeStruct((n_edges, width), BF),
            jax.ShapeDtypeStruct((feats, n_edges), BF),
        ),
        grid=(steps,),
        in_specs=[
            pl.BlockSpec((feats, eb), lambda i: (0, i)),
            full(w_up.shape),
            pl.BlockSpec((eb, width), lambda i: (i, 0)),
        ],
        out_specs=(
            pl.BlockSpec((eb, width), lambda i: (i, 0)),
            pl.BlockSpec((feats, eb), lambda i: (0, i)),
        ),
        compiler_params=params(),
        name="dense",
    )(agg_t, w_up, cot)


def backward_kernel(g_agg_t, src_t, ranges, trip, w_basis_t, peers, nb):
    feats, n_edges = g_agg_t.shape
    chunks, rows, _ = trip.shape
    per = 8
    steps = chunks // per
    eblocks = n_edges // LO

    def body(rg, g_ref, st_ref, x_ref, w_ref, out_ref, gb_out, table, acc, source):
        i = pl.program_id(0)

        @pl.when(i == 0)
        def _():
            acc[...] = jnp.zeros_like(acc)
            for j in range(eblocks):
                table[j * feats:(j + 1) * feats] = g_ref[:, j * LO:(j + 1) * LO]

        def ids(a, k):
            return x_ref[a, nb + k:nb + k + 1].astype(jnp.int32)

        far = jnp.int32(0)
        for a in range(per):
            g_trip = pick(nn(table[...], onehot(ids(a, 2), LO)), ids(a, 3), eblocks, feats)
            gb_out[a] = g_trip * st_ref[a].astype(F32)
            source[a] = g_trip * nn(w_ref[...], x_ref[a].astype(BF))
        for a in range(per):
            b0 = rg[0, i * per + a]
            far = jnp.maximum(far, rg[1, i * per + a] - b0)
            hot = onehot(ids(a, 0), LO)
            hi = ids(a, 1)
            for n in range(NEAR):
                res = nt(jnp.where(hi == b0 + n, source[a], 0.0).astype(BF), hot)
                acc[jnp.minimum(b0 + n, peers - 1)] += res

        @pl.when(far >= NEAR)
        def _():
            for a in range(per):
                def more(b, _, a=a):
                    part = jnp.where(ids(a, 1) == b, source[a], 0.0).astype(BF)
                    acc[b] += nt(part, onehot(ids(a, 0), LO))
                    return 0
                lax.fori_loop(rg[0, i * per + a] + NEAR, rg[1, i * per + a] + 1, more, 0)

        @pl.when(i == steps - 1)
        def _():
            out_ref[...] = acc[...].astype(BF)

    def whole(shape):
        return pl.BlockSpec(shape, lambda i, rg: (0,) * len(shape))

    return pl.pallas_call(
        body,
        out_shape=(
            jax.ShapeDtypeStruct((peers, feats, LO), BF),
            jax.ShapeDtypeStruct((chunks, feats, LO), F32),
        ),
        grid_spec=pltpu.PrefetchScalarGridSpec(
            num_scalar_prefetch=1,
            grid=(steps,),
            in_specs=[
                whole(g_agg_t.shape),
                pl.BlockSpec((per, feats, LO), lambda i, rg: (i, 0, 0)),
                pl.BlockSpec((per, rows, LO), lambda i, rg: (i, 0, 0)),
                whole(w_basis_t.shape),
            ],
            out_specs=(
                whole((peers, feats, LO)),
                pl.BlockSpec((per, feats, LO), lambda i, rg: (i, 0, 0)),
            ),
            scratch_shapes=[
                pltpu.VMEM((eblocks * feats, LO), BF),
                pltpu.VMEM((peers, feats, LO), F32),
                pltpu.VMEM((per, feats, LO), F32),
            ],
        ),
        compiler_params=params(),
        name="backward",
    )(ranges, g_agg_t, src_t, trip, w_basis_t)


def weights_kernel(agg_t, g_pre, g_basis, trip, fold):
    feats, n_edges = agg_t.shape
    width = g_pre.shape[1]
    chunks, rows, _ = trip.shape
    steps = 4
    eb = n_edges // steps
    per = chunks // steps
    per_row = width // fold

    def body(a_ref, p_ref, g_ref, x_ref, out_ref, up, bt):
        i = pl.program_id(0)

        @pl.when(i == 0)
        def _():
            up[...] = jnp.zeros_like(up)
            bt[...] = jnp.zeros_like(bt)

        up[...] += nn(a_ref[...], p_ref[...])
        for a in range(per):
            top = g_ref[a].astype(BF)
            low = (g_ref[a] - top.astype(F32)).astype(BF)
            basis = x_ref[a].astype(BF)
            bt[...] += nt(basis, top) + nt(basis, low)

        @pl.when(i == steps - 1)
        def _():
            for q in range(per_row):
                out_ref[:, q * feats:(q + 1) * feats] = up[:, q * fold:(q + 1) * fold].T.astype(BF)
            out_ref[:, per_row * feats:] = jnp.zeros((fold, feats), BF)
            out_ref[:rows, per_row * feats:] = bt[...].astype(BF)

    return pl.pallas_call(
        body,
        out_shape=jax.ShapeDtypeStruct((fold, (per_row + 1) * feats), BF),
        grid=(steps,),
        in_specs=[
            pl.BlockSpec((feats, eb), lambda i: (0, i)),
            pl.BlockSpec((eb, width), lambda i: (i, 0)),
            pl.BlockSpec((per, feats, LO), lambda i: (i, 0, 0)),
            pl.BlockSpec((per, rows, LO), lambda i: (i, 0, 0)),
        ],
        out_specs=full((fold, (per_row + 1) * feats)),
        scratch_shapes=[pltpu.VMEM((feats, width), F32), pltpu.VMEM((rows, feats), F32)],
        compiler_params=params(),
        name="weights",
    )(agg_t, g_pre, g_basis, trip)


def return_kernel(ret, send_idx, edges, small):
    peers, feats, slot = ret.shape
    n_edges, width = edges.shape
    fold = small.shape[0]
    lanes = width // fold * feats + small.shape[1]
    per = 8
    steps = peers // per
    eblocks = n_edges // LO
    eb = 512
    esteps = n_edges // eb

    def body(r_ref, i_ref, e_ref, s_ref, down_out, grad_out, acc, pm, oh, gacc):
        i = pl.program_id(0)

        @pl.when(i == 0)
        def _():
            acc[...] = jnp.zeros_like(acc)
            gacc[...] = jnp.zeros_like(gacc)

        @pl.when(i < steps)
        def _():
            for a in range(per):
                cols = slice(a * slot, (a + 1) * slot)
                lo, hi = split(i_ref[:, cols])
                rows = r_ref[a].astype(F32)
                for j in range(eblocks):
                    pm[j * feats:(j + 1) * feats, cols] = jnp.where(hi == j, rows, 0.0).astype(BF)
                oh[:, cols] = onehot(lo, slot)
            acc[...] += nt(pm[...], oh[...])

        @pl.when(i == steps - 1)
        def _():
            for j in range(eblocks):
                down_out[:, j * LO:(j + 1) * LO] = acc[j * feats:(j + 1) * feats].astype(BF)

        @pl.when(i >= steps)
        def _():
            k = i - steps
            gacc[...] += nn(down_out[:, pl.ds(pl.multiple_of(k * eb, eb), eb)], e_ref[...])

        @pl.when(i == steps + esteps - 1)
        def _():
            for q in range(width // fold):
                grad_out[:, q * feats:(q + 1) * feats] = gacc[:, q * fold:(q + 1) * fold].T.astype(BF)
            grad_out[:, width // fold * feats:] = s_ref[...]

    return pl.pallas_call(
        body,
        out_shape=(
            jax.ShapeDtypeStruct((feats, n_edges), BF),
            jax.ShapeDtypeStruct((fold, lanes), BF),
        ),
        grid=(steps + esteps,),
        in_specs=[
            pl.BlockSpec((per, feats, slot), lambda i: (jnp.minimum(i, steps - 1), 0, 0)),
            pl.BlockSpec((1, per * slot), lambda i: (0, jnp.minimum(i, steps - 1))),
            pl.BlockSpec((eb, width), lambda i: (jnp.maximum(i - steps, 0), 0)),
            full(small.shape),
        ],
        out_specs=(full((feats, n_edges)), full((fold, lanes))),
        scratch_shapes=[
            pltpu.VMEM((eblocks * feats, LO), F32),
            pltpu.VMEM((eblocks * feats, per * slot), BF),
            pltpu.VMEM((LO, per * slot), BF),
            pltpu.VMEM((feats, width), F32),
        ],
        compiler_params=params(),
        name="returned",
    )(ret, send_idx, edges, small)


def edges_kernel(g_down_t, w_down_t):
    feats, n_edges = g_down_t.shape
    width = w_down_t.shape[1]
    eb = 512

    def body(g_ref, w_ref, out_ref):
        out_ref[...] = tn(g_ref[...], w_ref[...]).astype(BF)

    return pl.pallas_call(
        body,
        out_shape=jax.ShapeDtypeStruct((n_edges, width), BF),
        grid=(n_edges // eb,),
        in_specs=[pl.BlockSpec((feats, eb), lambda i: (0, i)), full(w_down_t.shape)],
        out_specs=pl.BlockSpec((eb, width), lambda i: (i, 0)),
        compiler_params=params(),
        name="grad_edges",
    )(g_down_t, w_down_t)


def exchange(x, axes):
    return lax.all_to_all(x, axes, split_axis=0, concat_axis=0, tiled=True)


def reduce_all(x, n):
    rows, width = x.shape
    slab = (rows // n, width)
    mine = exchange(x.reshape((n,) + slab), ("dp", "graph")).astype(F32).sum(axis=0)
    spread = jnp.broadcast_to(mine.astype(BF)[None], (n,) + slab)
    return exchange(spread, ("dp", "graph")).reshape(rows, width)


def make_shards(n_dp, n_graph):
    def shards(edges, send_rows, trip_src, trip_dst, basis_values, cotangent, w_down, w_up, w_basis):
        edge_rows = edges[0]
        basis = basis_values[0]
        n_edges, width = edge_rows.shape
        feats = w_down.shape[1]
        nb = basis.shape[0]
        sent = send_kernel(edge_rows, w_down, send_rows, n_graph)
        received = exchange(sent, "graph")
        src, sent_now = lax.optimization_barrier((trip_src, sent))
        trip, ranges = sort_kernel(src, trip_dst, basis, n_graph)
        w_basis_t = jnp.pad(w_basis.T, ((0, 0), (0, trip.shape[1] - nb)))
        src_t, agg_t = forward_kernel(received, ranges, trip, w_basis_t, n_edges, nb)
        g_pre, g_agg_t = dense_kernel(agg_t, w_up, cotangent[0])
        g_received, g_basis = backward_kernel(
            g_agg_t, src_t, ranges, trip, w_basis_t, n_graph, nb
        )
        returned = exchange(g_received, "graph")
        small = weights_kernel(agg_t, g_pre, g_basis, trip, 2 * n_dp * n_graph)
        g_down_t, terms = return_kernel(returned, send_rows, edge_rows, small)
        reduced = reduce_all(terms, n_dp * n_graph)
        grad_edges = edges_kernel(g_down_t, w_down.T)
        fold = reduced.shape[0]
        parts = [reduced[:, k * feats:(k + 1) * feats] for k in range(reduced.shape[1] // feats)]
        per = width // fold
        grad_down = jnp.concatenate(parts[:per]).astype(F32)
        grad_up = jnp.concatenate(parts[per:2 * per]).astype(F32).T
        grad_basis = parts[2 * per][:nb].astype(F32)
        return grad_edges[None], grad_down, grad_up, grad_basis

    return shards


def solution(mesh):
    shape = dict(mesh.shape)
    in_specs = (
        P("dp", "graph", None),
        P("dp", "graph"),
        P("dp", "graph"),
        P("dp", "graph"),
        P("dp", None, "graph"),
        P("dp", "graph", None),
        P(),
        P(),
        P(),
    )
    out_specs = (P("dp", "graph", None), P(), P(), P())
    return jax.shard_map(
        make_shards(shape["dp"], shape["graph"]),
        mesh=mesh,
        in_specs=in_specs,
        out_specs=out_specs,
        check_vma=False,
    )
```

```python
import jax
import jax.numpy as jnp
from jax import lax
from jax.experimental import pallas as pl
from jax.experimental.pallas import tpu as pltpu
from jax.sharding import PartitionSpec as P

LO = 256
BF = jnp.bfloat16
F32 = jnp.float32


def split(idx):
    return idx & (LO - 1), idx >> 8


def onehot(lo, width):
    rows = lax.broadcasted_iota(jnp.int32, (LO, width), 0)
    return jnp.where(rows == lo, 1.0, 0.0).astype(BF)


def nn(a, b):
    return jnp.dot(a, b, preferred_element_type=F32)


def nt(a, b):
    return lax.dot_general(a, b, (((1,), (1,)), ((), ())), preferred_element_type=F32)


def tn(a, b):
    return lax.dot_general(a, b, (((0,), (0,)), ((), ())), preferred_element_type=F32)


def pick(res, hi, blocks, feats, base=0):
    acc = jnp.zeros((feats, res.shape[1]), F32)
    for j in range(blocks):
        acc = jnp.where(hi == base + j, res[j * feats:(j + 1) * feats], acc)
    return acc


def params():
    return pltpu.CompilerParams(vmem_limit_bytes=56 * 1024 * 1024)


def full(shape):
    return pl.BlockSpec(shape, lambda i: (0,) * len(shape))


def send_kernel(edges, w_down, send_idx, peers):
    n_edges, width = edges.shape
    feats = w_down.shape[1]
    eb = 1024
    nd = n_edges // eb
    per = 16
    ng = peers // per
    slot = send_idx.shape[1] // peers
    blocks = n_edges // LO

    def body(e_ref, w_ref, i_ref, out_ref, table):
        i = pl.program_id(0)

        @pl.when(i < nd)
        def _():
            d = nn(e_ref[...], w_ref[...]).astype(BF).T
            for k in range(eb // LO):
                table[i * (eb // LO) + k] = d[:, k * LO:(k + 1) * LO]

        @pl.when(i >= nd)
        def _():
            tab = table[...].reshape(blocks * feats, LO)
            for a in range(per):
                lo, hi = split(i_ref[:, a * slot:(a + 1) * slot])
                res = nn(tab, onehot(lo, slot))
                out_ref[a] = pick(res, hi, blocks, feats).astype(BF)

    return pl.pallas_call(
        body,
        out_shape=jax.ShapeDtypeStruct((peers, feats, slot), BF),
        grid=(nd + ng,),
        in_specs=[
            pl.BlockSpec((eb, width), lambda i: (jnp.minimum(i, nd - 1), 0)),
            full(w_down.shape),
            pl.BlockSpec((1, per * slot), lambda i: (0, jnp.maximum(i - nd, 0))),
        ],
        out_specs=pl.BlockSpec((per, feats, slot), lambda i: (jnp.maximum(i - nd, 0), 0, 0)),
        scratch_shapes=[pltpu.VMEM((blocks, feats, LO), BF)],
        compiler_params=params(),
        name="send",
    )(edges, w_down, send_idx)


def sort_kernel(src, dst, basis, peers):
    trips = src.shape[1]
    nb = basis.shape[0]
    rows = -(-(nb + 4) // 16) * 16
    chunks = trips // LO
    tc = 1024
    steps = trips // tc

    def body(s_ref, d_ref, b_ref, x_out, range_out, oh_hi, first, pm, oh, acc):
        i = pl.program_id(0)

        @pl.when(i == 0)
        def _():
            acc[...] = jnp.zeros_like(acc)
            bucket = lax.broadcasted_iota(jnp.int32, (peers, trips), 0)
            hot = jnp.where(bucket == (s_ref[...] >> 8), 1.0, 0.0)
            oh_hi[...] = hot.astype(BF)
            total = jnp.broadcast_to(jnp.sum(hot, axis=1, keepdims=True), (peers, 128))
            high = jnp.floor(total * (1.0 / 256.0))
            low = total - high * 256.0
            r = lax.broadcasted_iota(jnp.int32, (peers, peers), 0)
            c = lax.broadcasted_iota(jnp.int32, (peers, peers), 1)
            before = jnp.where(c < r, 1.0, 0.0).astype(BF)
            start = 256.0 * nn(before, high.astype(BF)) + nn(before, low.astype(BF))
            first[...] = start
            edge = 256.0 * lax.broadcasted_iota(jnp.int32, (peers, 128), 1).astype(F32)
            b0 = jnp.sum(jnp.where(start + total <= edge, 1.0, 0.0), axis=0, keepdims=True)
            b1 = jnp.sum(jnp.where(start < edge + 256.0, 1.0, 0.0), axis=0, keepdims=True) - 1.0
            range_out[0:1] = jnp.minimum(b0, peers - 1.0).astype(jnp.int32)
            range_out[1:2] = b1.astype(jnp.int32)

        r = lax.broadcasted_iota(jnp.int32, (LO, LO), 0)
        c = lax.broadcasted_iota(jnp.int32, (LO, LO), 1)
        upto = jnp.where(r <= c, 1.0, 0.0).astype(BF)
        for a in range(tc // LO):
            cols = slice(a * LO, (a + 1) * LO)
            at = pl.multiple_of(i * tc + a * LO, LO)
            hot = oh_hi[:, pl.ds(at, LO)]
            count = nn(hot, upto)
            place = first[:, 0:1] + count - 1.0
            hot32 = hot.astype(F32)
            pos = jnp.sum(hot32 * place, axis=0, keepdims=True).astype(jnp.int32)
            first[...] += jnp.broadcast_to(count[:, LO - 1:LO], first.shape)
            s_lo, s_hi = split(s_ref[:, pl.ds(at, LO)])
            d_lo, d_hi = split(d_ref[:, cols])
            row = lax.broadcasted_iota(jnp.int32, (rows - nb, LO), 0)
            extra = jnp.where(row == 0, s_lo, jnp.where(row == 1, s_hi, jnp.where(row == 2, d_lo, jnp.where(row == 3, d_hi, 0))))
            x = jnp.concatenate([b_ref[:, cols].astype(F32), extra.astype(F32)], axis=0)
            lo, hi = split(pos)
            for j in range(chunks):
                pm[j * rows:(j + 1) * rows, cols] = jnp.where(hi == j, x, 0.0).astype(BF)
            oh[:, cols] = onehot(lo, LO)
        acc[...] += nt(pm[...], oh[...])

        @pl.when(i == steps - 1)
        def _():
            x_out[...] = acc[...].reshape(x_out.shape)

    return pl.pallas_call(
        body,
        out_shape=(
            jax.ShapeDtypeStruct((chunks, rows, LO), F32),
            jax.ShapeDtypeStruct((2, 128), jnp.int32),
        ),
        grid=(steps,),
        in_specs=[
            full(src.shape),
            pl.BlockSpec((1, tc), lambda i: (0, i)),
            pl.BlockSpec((nb, tc), lambda i: (0, i)),
        ],
        out_specs=(full((chunks, rows, LO)), full((2, 128))),
        scratch_shapes=[
            pltpu.VMEM((peers, trips), BF),
            pltpu.VMEM((peers, 128), F32),
            pltpu.VMEM((chunks * rows, tc), BF),
            pltpu.VMEM((LO, tc), BF),
            pltpu.VMEM((chunks * rows, LO), F32),
        ],
        compiler_params=params(),
        name="order",
    )(src, dst, basis)


NEAR = 3


def forward_kernel(recv, ranges, trip, w_basis_t, n_edges, nb):
    peers, feats, _ = recv.shape
    chunks, rows, _ = trip.shape
    per = 16
    steps = chunks // per
    eblocks = n_edges // LO

    def body(rg, r_ref, x_ref, w_ref, src_out, agg_out, acc, pm, oh, source):
        i = pl.program_id(0)

        @pl.when(i == 0)
        def _():
            acc[...] = jnp.zeros_like(acc)

        def ids(a, k):
            return x_ref[a, nb + k:nb + k + 1].astype(jnp.int32)

        far = jnp.int32(0)
        for a in range(per):
            b0 = rg[0, i * per + a]
            far = jnp.maximum(far, rg[1, i * per + a] - b0)
            hot = onehot(ids(a, 0), LO)
            hi = ids(a, 1)
            got = jnp.zeros((feats, LO), F32)
            for n in range(NEAR):
                res = nn(r_ref[jnp.minimum(b0 + n, peers - 1)], hot)
                got = jnp.where(hi == b0 + n, res, got)
            source[a] = got

        @pl.when(far >= NEAR)
        def _():
            for a in range(per):
                def more(b, _, a=a):
                    res = nn(r_ref[b], onehot(ids(a, 0), LO))
                    source[a] = jnp.where(ids(a, 1) == b, res, source[a])
                    return 0
                lax.fori_loop(rg[0, i * per + a] + NEAR, rg[1, i * per + a] + 1, more, 0)

        for a in range(per):
            cols = slice(a * LO, (a + 1) * LO)
            src_out[a] = source[a].astype(BF)
            product = source[a] * nn(w_ref[...], x_ref[a].astype(BF))
            hi = ids(a, 3)
            for j in range(eblocks):
                pm[j * feats:(j + 1) * feats, cols] = jnp.where(hi == j, product, 0.0).astype(BF)
            oh[:, cols] = onehot(ids(a, 2), LO)
        acc[...] += nt(pm[...], oh[...])

        @pl.when(i == steps - 1)
        def _():
            for j in range(eblocks):
                agg_out[:, j * LO:(j + 1) * LO] = acc[j * feats:(j + 1) * feats].astype(BF)

    def whole(shape):
        return pl.BlockSpec(shape, lambda i, rg: (0,) * len(shape))

    return pl.pallas_call(
        body,
        out_shape=(
            jax.ShapeDtypeStruct((chunks, feats, LO), BF),
            jax.ShapeDtypeStruct((feats, n_edges), BF),
        ),
        grid_spec=pltpu.PrefetchScalarGridSpec(
            num_scalar_prefetch=1,
            grid=(steps,),
            in_specs=[
                whole(recv.shape),
                pl.BlockSpec((per, rows, LO), lambda i, rg: (i, 0, 0)),
                whole(w_basis_t.shape),
            ],
            out_specs=(
                pl.BlockSpec((per, feats, LO), lambda i, rg: (i, 0, 0)),
                whole((feats, n_edges)),
            ),
            scratch_shapes=[
                pltpu.VMEM((eblocks * feats, LO), F32),
                pltpu.VMEM((eblocks * feats, per * LO), BF),
                pltpu.VMEM((LO, per * LO), BF),
                pltpu.VMEM((per, feats, LO), F32),
            ],
        ),
        compiler_params=params(),
        name="forward",
    )(ranges, recv, trip, w_basis_t)


def dense_kernel(agg_t, w_up, cot):
    feats, n_edges = agg_t.shape
    width = w_up.shape[1]
    eb = 1024
    steps = n_edges // eb

    def body(a_ref, w_ref, c_ref, p_out, g_out):
        for k in range(eb // 256):
            r = slice(k * 256, (k + 1) * 256)
            pre = tn(a_ref[:, r], w_ref[...])
            t = 0.5 * jnp.tanh(0.5 * pre)
            g_pre = (c_ref[r].astype(F32) * (0.5 + t) * (1.0 + pre * (0.5 - t))).astype(BF)
            p_out[r] = g_pre
            g_out[:, r] = nt(w_ref[...], g_pre).astype(BF)

    return pl.pallas_call(
        body,
        out_shape=(
            jax.ShapeDtypeStruct((n_edges, width), BF),
            jax.ShapeDtypeStruct((feats, n_edges), BF),
        ),
        grid=(steps,),
        in_specs=[
            pl.BlockSpec((feats, eb), lambda i: (0, i)),
            full(w_up.shape),
            pl.BlockSpec((eb, width), lambda i: (i, 0)),
        ],
        out_specs=(
            pl.BlockSpec((eb, width), lambda i: (i, 0)),
            pl.BlockSpec((feats, eb), lambda i: (0, i)),
        ),
        compiler_params=params(),
        name="dense",
    )(agg_t, w_up, cot)


def backward_kernel(g_agg_t, src_t, ranges, trip, w_basis_t, peers, nb):
    feats, n_edges = g_agg_t.shape
    chunks, rows, _ = trip.shape
    per = 8
    steps = chunks // per
    eblocks = n_edges // LO

    def body(rg, g_ref, st_ref, x_ref, w_ref, out_ref, gb_out, table, acc, source):
        i = pl.program_id(0)

        @pl.when(i == 0)
        def _():
            acc[...] = jnp.zeros_like(acc)
            for j in range(eblocks):
                table[j * feats:(j + 1) * feats] = g_ref[:, j * LO:(j + 1) * LO]

        def ids(a, k):
            return x_ref[a, nb + k:nb + k + 1].astype(jnp.int32)

        far = jnp.int32(0)
        for a in range(per):
            g_trip = pick(nn(table[...], onehot(ids(a, 2), LO)), ids(a, 3), eblocks, feats)
            gb_out[a] = g_trip * st_ref[a].astype(F32)
            source[a] = g_trip * nn(w_ref[...], x_ref[a].astype(BF))
        for a in range(per):
            b0 = rg[0, i * per + a]
            far = jnp.maximum(far, rg[1, i * per + a] - b0)
            hot = onehot(ids(a, 0), LO)
            hi = ids(a, 1)
            for n in range(NEAR):
                res = nt(jnp.where(hi == b0 + n, source[a], 0.0).astype(BF), hot)
                acc[jnp.minimum(b0 + n, peers - 1)] += res

        @pl.when(far >= NEAR)
        def _():
            for a in range(per):
                def more(b, _, a=a):
                    part = jnp.where(ids(a, 1) == b, source[a], 0.0).astype(BF)
                    acc[b] += nt(part, onehot(ids(a, 0), LO))
                    return 0
                lax.fori_loop(rg[0, i * per + a] + NEAR, rg[1, i * per + a] + 1, more, 0)

        @pl.when(i == steps - 1)
        def _():
            out_ref[...] = acc[...].astype(BF)

    def whole(shape):
        return pl.BlockSpec(shape, lambda i, rg: (0,) * len(shape))

    return pl.pallas_call(
        body,
        out_shape=(
            jax.ShapeDtypeStruct((peers, feats, LO), BF),
            jax.ShapeDtypeStruct((chunks, feats, LO), F32),
        ),
        grid_spec=pltpu.PrefetchScalarGridSpec(
            num_scalar_prefetch=1,
            grid=(steps,),
            in_specs=[
                whole(g_agg_t.shape),
                pl.BlockSpec((per, feats, LO), lambda i, rg: (i, 0, 0)),
                pl.BlockSpec((per, rows, LO), lambda i, rg: (i, 0, 0)),
                whole(w_basis_t.shape),
            ],
            out_specs=(
                whole((peers, feats, LO)),
                pl.BlockSpec((per, feats, LO), lambda i, rg: (i, 0, 0)),
            ),
            scratch_shapes=[
                pltpu.VMEM((eblocks * feats, LO), BF),
                pltpu.VMEM((peers, feats, LO), F32),
                pltpu.VMEM((per, feats, LO), F32),
            ],
        ),
        compiler_params=params(),
        name="backward",
    )(ranges, g_agg_t, src_t, trip, w_basis_t)


def weights_kernel(agg_t, g_pre, g_basis, trip, lines):
    feats, n_edges = agg_t.shape
    width = g_pre.shape[1]
    chunks, rows, _ = trip.shape
    steps = 4
    eb = n_edges // steps
    per = chunks // steps

    def body(a_ref, p_ref, g_ref, x_ref, out_ref, up, bt):
        i = pl.program_id(0)

        @pl.when(i == 0)
        def _():
            up[...] = jnp.zeros_like(up)
            bt[...] = jnp.zeros_like(bt)

        up[...] += nn(a_ref[...], p_ref[...])
        for a in range(per):
            top = g_ref[a].astype(BF)
            low = (g_ref[a] - top.astype(F32)).astype(BF)
            basis = x_ref[a].astype(BF)
            bt[...] += nt(basis, top) + nt(basis, low)

        @pl.when(i == steps - 1)
        def _():
            out_ref[:, :width] = up[...]
            tall = jnp.concatenate([bt[...], jnp.zeros((lines - rows, feats), F32)])
            out_ref[:, width:] = tall.T

    return pl.pallas_call(
        body,
        out_shape=jax.ShapeDtypeStruct((feats, width + lines), F32),
        grid=(steps,),
        in_specs=[
            pl.BlockSpec((feats, eb), lambda i: (0, i)),
            pl.BlockSpec((eb, width), lambda i: (i, 0)),
            pl.BlockSpec((per, feats, LO), lambda i: (i, 0, 0)),
            pl.BlockSpec((per, rows, LO), lambda i: (i, 0, 0)),
        ],
        out_specs=full((feats, width + lines)),
        scratch_shapes=[pltpu.VMEM((feats, width), F32), pltpu.VMEM((rows, feats), F32)],
        compiler_params=params(),
        name="weights",
    )(agg_t, g_pre, g_basis, trip)


def return_kernel(ret, send_idx, edges, piece):
    peers, feats, slot = ret.shape
    n_edges, width = edges.shape
    fold = piece.shape[0]
    lanes = width // fold * feats + piece.shape[1]
    per = 32
    steps = peers // per
    eblocks = n_edges // LO
    eb = 2048
    esteps = n_edges // eb

    def body(r_ref, i_ref, e_ref, p_ref, down_out, grad_out, acc, pm, oh, gacc):
        i = pl.program_id(0)

        @pl.when(i == 0)
        def _():
            acc[...] = jnp.zeros_like(acc)
            gacc[...] = jnp.zeros_like(gacc)

        @pl.when(i < steps)
        def _():
            for a in range(per):
                cols = slice(a * slot, (a + 1) * slot)
                lo, hi = split(i_ref[:, cols])
                rows = r_ref[a].astype(F32)
                for j in range(eblocks):
                    pm[j * feats:(j + 1) * feats, cols] = jnp.where(hi == j, rows, 0.0).astype(BF)
                oh[:, cols] = onehot(lo, slot)
            acc[...] += nt(pm[...], oh[...])

        @pl.when(i == steps - 1)
        def _():
            for j in range(eblocks):
                down_out[:, j * LO:(j + 1) * LO] = acc[j * feats:(j + 1) * feats].astype(BF)

        @pl.when(i >= steps)
        def _():
            k = i - steps
            gacc[...] += nn(down_out[:, pl.ds(pl.multiple_of(k * eb, eb), eb)], e_ref[...])

        @pl.when(i == steps + esteps - 1)
        def _():
            for q in range(width // fold):
                grad_out[:, q * feats:(q + 1) * feats] = gacc[:, q * fold:(q + 1) * fold].T.astype(BF)
            grad_out[:, width // fold * feats:] = p_ref[...]

    return pl.pallas_call(
        body,
        out_shape=(
            jax.ShapeDtypeStruct((feats, n_edges), BF),
            jax.ShapeDtypeStruct((fold, lanes), BF),
        ),
        grid=(steps + esteps,),
        in_specs=[
            pl.BlockSpec((per, feats, slot), lambda i: (jnp.minimum(i, steps - 1), 0, 0)),
            pl.BlockSpec((1, per * slot), lambda i: (0, jnp.minimum(i, steps - 1))),
            pl.BlockSpec((eb, width), lambda i: (jnp.maximum(i - steps, 0), 0)),
            full(piece.shape),
        ],
        out_specs=(full((feats, n_edges)), full((fold, lanes))),
        scratch_shapes=[
            pltpu.VMEM((eblocks * feats, LO), F32),
            pltpu.VMEM((eblocks * feats, per * slot), BF),
            pltpu.VMEM((LO, per * slot), BF),
            pltpu.VMEM((feats, width), F32),
        ],
        compiler_params=params(),
        name="returned",
    )(ret, send_idx, edges, piece)


def edges_kernel(g_down_t, w_down_t):
    feats, n_edges = g_down_t.shape
    width = w_down_t.shape[1]
    eb = 1024

    def body(g_ref, w_ref, out_ref):
        out_ref[...] = tn(g_ref[...], w_ref[...]).astype(BF)

    return pl.pallas_call(
        body,
        out_shape=jax.ShapeDtypeStruct((n_edges, width), BF),
        grid=(n_edges // eb,),
        in_specs=[pl.BlockSpec((feats, eb), lambda i: (0, i)), full(w_down_t.shape)],
        out_specs=pl.BlockSpec((eb, width), lambda i: (i, 0)),
        compiler_params=params(),
        name="grad_edges",
    )(g_down_t, w_down_t)


def exchange(x, axes):
    return lax.all_to_all(x, axes, split_axis=0, concat_axis=0, tiled=True)


def total_kernel(got, n_dp, feats, own):
    n, pair, lanes = got.shape
    share = feats // n_dp
    groups = (lanes - own) // feats * 3
    out_lanes = own + groups * feats

    def body(x_ref, out_ref):
        sums = jnp.sum(x_ref[...].astype(F32).reshape(n_dp, n // n_dp, pair, lanes), axis=1)
        parts = [jnp.sum(sums[:, :, :own], axis=0)]
        where = lax.broadcasted_iota(jnp.int32, (n_dp, pair, feats), 2) // share
        mine = where == lax.broadcasted_iota(jnp.int32, (n_dp, pair, feats), 0)
        for q in range(groups):
            piece = sums[:, :, own + q * share:own + (q + 1) * share]
            wide = jnp.concatenate([piece] * n_dp, axis=2)
            parts.append(jnp.sum(jnp.where(mine, wide, 0.0), axis=0))
        row = jnp.concatenate(parts, axis=1).astype(BF)
        out_ref[...] = jnp.broadcast_to(row[None], out_ref.shape)

    return pl.pallas_call(
        body,
        out_shape=jax.ShapeDtypeStruct((n, pair, out_lanes), BF),
        compiler_params=params(),
        name="totals",
    )(got)


def share_out(part, fold):
    share, cols = part.shape
    tall = jnp.pad(part.T.astype(BF), ((0, -cols % fold), (0, 0)))
    wide = jnp.concatenate([tall[k:k + fold] for k in range(0, tall.shape[0], fold)], axis=1)
    return jnp.pad(wide, ((0, 0), (0, -wide.shape[1] % 128)))


def reduce_all(slab, n_dp, n_graph, feats, own):
    n = n_dp * n_graph
    axes = ("dp", "graph")
    got = exchange(slab.reshape(n, slab.shape[0] // n, slab.shape[1]), axes)
    sent = total_kernel(got, n_dp, feats, own)
    return exchange(sent, axes).reshape(slab.shape[0], sent.shape[2])


def make_shards(n_dp, n_graph):
    def shards(edges, send_rows, trip_src, trip_dst, basis_values, cotangent, w_down, w_up, w_basis):
        edge_rows = edges[0]
        basis = basis_values[0]
        n_edges, width = edge_rows.shape
        feats = w_down.shape[1]
        nb = basis.shape[0]
        sent = send_kernel(edge_rows, w_down, send_rows, n_graph)
        received = exchange(sent, "graph")
        src, sent_now = lax.optimization_barrier((trip_src, sent))
        trip, ranges = sort_kernel(src, trip_dst, basis, n_graph)
        w_basis_t = jnp.pad(w_basis.T, ((0, 0), (0, trip.shape[1] - nb)))
        src_t, agg_t = forward_kernel(received, ranges, trip, w_basis_t, n_edges, nb)
        g_pre, g_agg_t = dense_kernel(agg_t, w_up, cotangent[0])
        g_received, g_basis = backward_kernel(
            g_agg_t, src_t, ranges, trip, w_basis_t, n_graph, nb
        )
        returned = exchange(g_received, "graph")
        n = n_dp * n_graph
        fold = 2 * n
        small = weights_kernel(agg_t, g_pre, g_basis, trip, n)
        part = lax.psum_scatter(small, "dp", scatter_dimension=0, tiled=True)
        returned, piece = lax.optimization_barrier((returned, share_out(part, fold)))
        g_down_t, slab = return_kernel(returned, send_rows, edge_rows, piece)
        reduced = reduce_all(slab, n_dp, n_graph, feats, width // fold * feats)
        grad_edges = edges_kernel(g_down_t, w_down.T)
        parts = [reduced[:, k * feats:(k + 1) * feats] for k in range(reduced.shape[1] // feats)]
        per = width // fold
        grad_down = jnp.concatenate(parts[:per]).astype(F32)
        grad_up = jnp.concatenate(parts[per:2 * per]).astype(F32).T
        grad_basis = parts[2 * per][:nb].astype(F32)
        return grad_edges[None], grad_down, grad_up, grad_basis

    return shards


def solution(mesh):
    shape = dict(mesh.shape)
    in_specs = (
        P("dp", "graph", None),
        P("dp", "graph"),
        P("dp", "graph"),
        P("dp", "graph"),
        P("dp", None, "graph"),
        P("dp", "graph", None),
        P(),
        P(),
        P(),
    )
    out_specs = (P("dp", "graph", None), P(), P(), P())
    return jax.shard_map(
        make_shards(shape["dp"], shape["graph"]),
        mesh=mesh,
        in_specs=in_specs,
        out_specs=out_specs,
        check_vma=False,
    )
```

```python
import jax
import jax.numpy as jnp
from jax import lax
from jax.experimental import pallas as pl
from jax.experimental.pallas import tpu as pltpu
from jax.sharding import PartitionSpec as P

LO = 256
BF = jnp.bfloat16
F32 = jnp.float32


def split(idx):
    return idx & (LO - 1), idx >> 8


def onehot(lo, width):
    rows = lax.broadcasted_iota(jnp.int32, (LO, width), 0)
    return jnp.where(rows == lo, 1.0, 0.0).astype(BF)


def nn(a, b):
    return jnp.dot(a, b, preferred_element_type=F32)


def nt(a, b):
    return lax.dot_general(a, b, (((1,), (1,)), ((), ())), preferred_element_type=F32)


def tn(a, b):
    return lax.dot_general(a, b, (((0,), (0,)), ((), ())), preferred_element_type=F32)


def pick(res, hi, blocks, feats, base=0):
    acc = jnp.zeros((feats, res.shape[1]), F32)
    for j in range(blocks):
        acc = jnp.where(hi == base + j, res[j * feats:(j + 1) * feats], acc)
    return acc


def params():
    return pltpu.CompilerParams(vmem_limit_bytes=56 * 1024 * 1024)


def full(shape):
    return pl.BlockSpec(shape, lambda i: (0,) * len(shape))


def send_kernel(edges, w_down, send_idx, peers):
    n_edges, width = edges.shape
    feats = w_down.shape[1]
    eb = 1024
    nd = n_edges // eb
    per = 16
    ng = peers // per
    slot = send_idx.shape[1] // peers
    blocks = n_edges // LO

    def body(e_ref, w_ref, i_ref, out_ref, table):
        i = pl.program_id(0)

        @pl.when(i < nd)
        def _():
            d = nn(e_ref[...], w_ref[...]).astype(BF).T
            for k in range(eb // LO):
                table[i * (eb // LO) + k] = d[:, k * LO:(k + 1) * LO]

        @pl.when(i >= nd)
        def _():
            tab = table[...].reshape(blocks * feats, LO)
            for a in range(per):
                lo, hi = split(i_ref[:, a * slot:(a + 1) * slot])
                res = nn(tab, onehot(lo, slot))
                out_ref[a] = pick(res, hi, blocks, feats).astype(BF)

    return pl.pallas_call(
        body,
        out_shape=jax.ShapeDtypeStruct((peers, feats, slot), BF),
        grid=(nd + ng,),
        in_specs=[
            pl.BlockSpec((eb, width), lambda i: (jnp.minimum(i, nd - 1), 0)),
            full(w_down.shape),
            pl.BlockSpec((1, per * slot), lambda i: (0, jnp.maximum(i - nd, 0))),
        ],
        out_specs=pl.BlockSpec((per, feats, slot), lambda i: (jnp.maximum(i - nd, 0), 0, 0)),
        scratch_shapes=[pltpu.VMEM((blocks, feats, LO), BF)],
        compiler_params=params(),
        name="send",
    )(edges, w_down, send_idx)


def sort_kernel(src, dst, basis, peers):
    trips = src.shape[1]
    nb = basis.shape[0]
    rows = -(-(nb + 4) // 16) * 16
    chunks = trips // LO
    tc = 1024
    steps = trips // tc

    def body(s_ref, d_ref, b_ref, x_out, range_out, oh_hi, first, pm, oh, acc):
        i = pl.program_id(0)

        @pl.when(i == 0)
        def _():
            acc[...] = jnp.zeros_like(acc)
            bucket = lax.broadcasted_iota(jnp.int32, (peers, trips), 0)
            hot = jnp.where(bucket == (s_ref[...] >> 8), 1.0, 0.0)
            oh_hi[...] = hot.astype(BF)
            total = jnp.broadcast_to(jnp.sum(hot, axis=1, keepdims=True), (peers, 128))
            high = jnp.floor(total * (1.0 / 256.0))
            low = total - high * 256.0
            r = lax.broadcasted_iota(jnp.int32, (peers, peers), 0)
            c = lax.broadcasted_iota(jnp.int32, (peers, peers), 1)
            before = jnp.where(c < r, 1.0, 0.0).astype(BF)
            start = 256.0 * nn(before, high.astype(BF)) + nn(before, low.astype(BF))
            first[...] = start
            edge = 256.0 * lax.broadcasted_iota(jnp.int32, (peers, 128), 1).astype(F32)
            b0 = jnp.sum(jnp.where(start + total <= edge, 1.0, 0.0), axis=0, keepdims=True)
            b1 = jnp.sum(jnp.where(start < edge + 256.0, 1.0, 0.0), axis=0, keepdims=True) - 1.0
            range_out[0:1] = jnp.minimum(b0, peers - 1.0).astype(jnp.int32)
            range_out[1:2] = b1.astype(jnp.int32)

        r = lax.broadcasted_iota(jnp.int32, (LO, LO), 0)
        c = lax.broadcasted_iota(jnp.int32, (LO, LO), 1)
        upto = jnp.where(r <= c, 1.0, 0.0).astype(BF)
        for a in range(tc // LO):
            cols = slice(a * LO, (a + 1) * LO)
            at = pl.multiple_of(i * tc + a * LO, LO)
            hot = oh_hi[:, pl.ds(at, LO)]
            count = nn(hot, upto)
            place = first[:, 0:1] + count - 1.0
            hot32 = hot.astype(F32)
            pos = jnp.sum(hot32 * place, axis=0, keepdims=True).astype(jnp.int32)
            first[...] += jnp.broadcast_to(count[:, LO - 1:LO], first.shape)
            s_lo, s_hi = split(s_ref[:, pl.ds(at, LO)])
            d_lo, d_hi = split(d_ref[:, cols])
            row = lax.broadcasted_iota(jnp.int32, (rows - nb, LO), 0)
            extra = jnp.where(row == 0, s_lo, jnp.where(row == 1, s_hi, jnp.where(row == 2, d_lo, jnp.where(row == 3, d_hi, 0))))
            x = jnp.concatenate([b_ref[:, cols].astype(F32), extra.astype(F32)], axis=0)
            lo, hi = split(pos)
            for j in range(chunks):
                pm[j * rows:(j + 1) * rows, cols] = jnp.where(hi == j, x, 0.0).astype(BF)
            oh[:, cols] = onehot(lo, LO)
        acc[...] += nt(pm[...], oh[...])

        @pl.when(i == steps - 1)
        def _():
            x_out[...] = acc[...].reshape(x_out.shape)

    return pl.pallas_call(
        body,
        out_shape=(
            jax.ShapeDtypeStruct((chunks, rows, LO), F32),
            jax.ShapeDtypeStruct((2, 128), jnp.int32),
        ),
        grid=(steps,),
        in_specs=[
            full(src.shape),
            pl.BlockSpec((1, tc), lambda i: (0, i)),
            pl.BlockSpec((nb, tc), lambda i: (0, i)),
        ],
        out_specs=(full((chunks, rows, LO)), full((2, 128))),
        scratch_shapes=[
            pltpu.VMEM((peers, trips), BF),
            pltpu.VMEM((peers, 128), F32),
            pltpu.VMEM((chunks * rows, tc), BF),
            pltpu.VMEM((LO, tc), BF),
            pltpu.VMEM((chunks * rows, LO), F32),
        ],
        compiler_params=params(),
        name="order",
    )(src, dst, basis)


NEAR = 3


def forward_kernel(recv, ranges, trip, w_basis_t, n_edges, nb):
    peers, feats, _ = recv.shape
    chunks, rows, _ = trip.shape
    per = 16
    steps = chunks // per
    eblocks = n_edges // LO

    def body(rg, r_ref, x_ref, w_ref, src_out, agg_out, acc, pm, oh, source):
        i = pl.program_id(0)

        @pl.when(i == 0)
        def _():
            acc[...] = jnp.zeros_like(acc)

        def ids(a, k):
            return x_ref[a, nb + k:nb + k + 1].astype(jnp.int32)

        far = jnp.int32(0)
        for a in range(per):
            b0 = rg[0, i * per + a]
            far = jnp.maximum(far, rg[1, i * per + a] - b0)
            hot = onehot(ids(a, 0), LO)
            hi = ids(a, 1)
            got = jnp.zeros((feats, LO), F32)
            for n in range(NEAR):
                res = nn(r_ref[jnp.minimum(b0 + n, peers - 1)], hot)
                got = jnp.where(hi == b0 + n, res, got)
            source[a] = got

        @pl.when(far >= NEAR)
        def _():
            for a in range(per):
                def more(b, _, a=a):
                    res = nn(r_ref[b], onehot(ids(a, 0), LO))
                    source[a] = jnp.where(ids(a, 1) == b, res, source[a])
                    return 0
                lax.fori_loop(rg[0, i * per + a] + NEAR, rg[1, i * per + a] + 1, more, 0)

        for a in range(per):
            cols = slice(a * LO, (a + 1) * LO)
            src_out[a] = source[a].astype(BF)
            product = source[a] * nn(w_ref[...], x_ref[a].astype(BF))
            hi = ids(a, 3)
            for j in range(eblocks):
                pm[j * feats:(j + 1) * feats, cols] = jnp.where(hi == j, product, 0.0).astype(BF)
            oh[:, cols] = onehot(ids(a, 2), LO)
        acc[...] += nt(pm[...], oh[...])

        @pl.when(i == steps - 1)
        def _():
            for j in range(eblocks):
                agg_out[:, j * LO:(j + 1) * LO] = acc[j * feats:(j + 1) * feats].astype(BF)

    def whole(shape):
        return pl.BlockSpec(shape, lambda i, rg: (0,) * len(shape))

    return pl.pallas_call(
        body,
        out_shape=(
            jax.ShapeDtypeStruct((chunks, feats, LO), BF),
            jax.ShapeDtypeStruct((feats, n_edges), BF),
        ),
        grid_spec=pltpu.PrefetchScalarGridSpec(
            num_scalar_prefetch=1,
            grid=(steps,),
            in_specs=[
                whole(recv.shape),
                pl.BlockSpec((per, rows, LO), lambda i, rg: (i, 0, 0)),
                whole(w_basis_t.shape),
            ],
            out_specs=(
                pl.BlockSpec((per, feats, LO), lambda i, rg: (i, 0, 0)),
                whole((feats, n_edges)),
            ),
            scratch_shapes=[
                pltpu.VMEM((eblocks * feats, LO), F32),
                pltpu.VMEM((eblocks * feats, per * LO), BF),
                pltpu.VMEM((LO, per * LO), BF),
                pltpu.VMEM((per, feats, LO), F32),
            ],
        ),
        compiler_params=params(),
        name="forward",
    )(ranges, recv, trip, w_basis_t)


def dense_kernel(agg_t, w_up, cot):
    feats, n_edges = agg_t.shape
    width = w_up.shape[1]
    eb = 1024
    steps = n_edges // eb

    def body(a_ref, w_ref, c_ref, p_out, g_out):
        for k in range(eb // 256):
            r = slice(k * 256, (k + 1) * 256)
            pre = tn(a_ref[:, r], w_ref[...])
            t = 0.5 * jnp.tanh(0.5 * pre)
            g_pre = (c_ref[r].astype(F32) * (0.5 + t) * (1.0 + pre * (0.5 - t))).astype(BF)
            p_out[r] = g_pre
            g_out[:, r] = nt(w_ref[...], g_pre).astype(BF)

    return pl.pallas_call(
        body,
        out_shape=(
            jax.ShapeDtypeStruct((n_edges, width), BF),
            jax.ShapeDtypeStruct((feats, n_edges), BF),
        ),
        grid=(steps,),
        in_specs=[
            pl.BlockSpec((feats, eb), lambda i: (0, i)),
            full(w_up.shape),
            pl.BlockSpec((eb, width), lambda i: (i, 0)),
        ],
        out_specs=(
            pl.BlockSpec((eb, width), lambda i: (i, 0)),
            pl.BlockSpec((feats, eb), lambda i: (0, i)),
        ),
        compiler_params=params(),
        name="dense",
    )(agg_t, w_up, cot)


def backward_kernel(g_agg_t, src_t, ranges, trip, w_basis_t, peers, nb):
    feats, n_edges = g_agg_t.shape
    chunks, rows, _ = trip.shape
    per = 8
    steps = chunks // per
    eblocks = n_edges // LO

    def body(rg, g_ref, st_ref, x_ref, w_ref, out_ref, gb_out, table, acc, source):
        i = pl.program_id(0)

        @pl.when(i == 0)
        def _():
            acc[...] = jnp.zeros_like(acc)
            for j in range(eblocks):
                table[j * feats:(j + 1) * feats] = g_ref[:, j * LO:(j + 1) * LO]

        def ids(a, k):
            return x_ref[a, nb + k:nb + k + 1].astype(jnp.int32)

        far = jnp.int32(0)
        for a in range(per):
            g_trip = pick(nn(table[...], onehot(ids(a, 2), LO)), ids(a, 3), eblocks, feats)
            gb_out[a] = g_trip * st_ref[a].astype(F32)
            source[a] = g_trip * nn(w_ref[...], x_ref[a].astype(BF))
        for a in range(per):
            b0 = rg[0, i * per + a]
            far = jnp.maximum(far, rg[1, i * per + a] - b0)
            hot = onehot(ids(a, 0), LO)
            hi = ids(a, 1)
            for n in range(NEAR):
                res = nt(jnp.where(hi == b0 + n, source[a], 0.0).astype(BF), hot)
                acc[jnp.minimum(b0 + n, peers - 1)] += res

        @pl.when(far >= NEAR)
        def _():
            for a in range(per):
                def more(b, _, a=a):
                    part = jnp.where(ids(a, 1) == b, source[a], 0.0).astype(BF)
                    acc[b] += nt(part, onehot(ids(a, 0), LO))
                    return 0
                lax.fori_loop(rg[0, i * per + a] + NEAR, rg[1, i * per + a] + 1, more, 0)

        @pl.when(i == steps - 1)
        def _():
            out_ref[...] = acc[...].astype(BF)

    def whole(shape):
        return pl.BlockSpec(shape, lambda i, rg: (0,) * len(shape))

    return pl.pallas_call(
        body,
        out_shape=(
            jax.ShapeDtypeStruct((peers, feats, LO), BF),
            jax.ShapeDtypeStruct((chunks, feats, LO), F32),
        ),
        grid_spec=pltpu.PrefetchScalarGridSpec(
            num_scalar_prefetch=1,
            grid=(steps,),
            in_specs=[
                whole(g_agg_t.shape),
                pl.BlockSpec((per, feats, LO), lambda i, rg: (i, 0, 0)),
                pl.BlockSpec((per, rows, LO), lambda i, rg: (i, 0, 0)),
                whole(w_basis_t.shape),
            ],
            out_specs=(
                whole((peers, feats, LO)),
                pl.BlockSpec((per, feats, LO), lambda i, rg: (i, 0, 0)),
            ),
            scratch_shapes=[
                pltpu.VMEM((eblocks * feats, LO), BF),
                pltpu.VMEM((peers, feats, LO), F32),
                pltpu.VMEM((per, feats, LO), F32),
            ],
        ),
        compiler_params=params(),
        name="backward",
    )(ranges, g_agg_t, src_t, trip, w_basis_t)


def weights_kernel(agg_t, g_pre, g_basis, trip, lines):
    feats, n_edges = agg_t.shape
    width = g_pre.shape[1]
    chunks, rows, _ = trip.shape
    steps = 4
    eb = n_edges // steps
    per = chunks // steps

    def body(a_ref, p_ref, g_ref, x_ref, out_ref, up, bt):
        i = pl.program_id(0)

        @pl.when(i == 0)
        def _():
            up[...] = jnp.zeros_like(up)
            bt[...] = jnp.zeros_like(bt)

        up[...] += nn(a_ref[...], p_ref[...])
        for a in range(per):
            top = g_ref[a].astype(BF)
            low = (g_ref[a] - top.astype(F32)).astype(BF)
            basis = x_ref[a].astype(BF)
            bt[...] += nt(basis, top) + nt(basis, low)

        @pl.when(i == steps - 1)
        def _():
            out_ref[:, :width] = up[...]
            tall = jnp.concatenate([bt[...], jnp.zeros((lines - rows, feats), F32)])
            out_ref[:, width:] = tall.T

    return pl.pallas_call(
        body,
        out_shape=jax.ShapeDtypeStruct((feats, width + lines), F32),
        grid=(steps,),
        in_specs=[
            pl.BlockSpec((feats, eb), lambda i: (0, i)),
            pl.BlockSpec((eb, width), lambda i: (i, 0)),
            pl.BlockSpec((per, feats, LO), lambda i: (i, 0, 0)),
            pl.BlockSpec((per, rows, LO), lambda i: (i, 0, 0)),
        ],
        out_specs=full((feats, width + lines)),
        scratch_shapes=[pltpu.VMEM((feats, width), F32), pltpu.VMEM((rows, feats), F32)],
        compiler_params=params(),
        name="weights",
    )(agg_t, g_pre, g_basis, trip)


def return_kernel(ret, send_idx, edges, piece):
    peers, feats, slot = ret.shape
    n_edges, width = edges.shape
    fold = piece.shape[0]
    lanes = width // fold * feats + piece.shape[1]
    per = 32
    steps = peers // per
    eblocks = n_edges // LO
    eb = 2048
    esteps = n_edges // eb

    def body(r_ref, i_ref, e_ref, p_ref, down_out, grad_out, acc, pm, oh, gacc):
        i = pl.program_id(0)

        @pl.when(i == 0)
        def _():
            acc[...] = jnp.zeros_like(acc)
            gacc[...] = jnp.zeros_like(gacc)

        @pl.when(i < steps)
        def _():
            for a in range(per):
                cols = slice(a * slot, (a + 1) * slot)
                lo, hi = split(i_ref[:, cols])
                rows = r_ref[a].astype(F32)
                for j in range(eblocks):
                    pm[j * feats:(j + 1) * feats, cols] = jnp.where(hi == j, rows, 0.0).astype(BF)
                oh[:, cols] = onehot(lo, slot)
            acc[...] += nt(pm[...], oh[...])

        @pl.when(i == steps - 1)
        def _():
            for j in range(eblocks):
                down_out[:, j * LO:(j + 1) * LO] = acc[j * feats:(j + 1) * feats].astype(BF)

        @pl.when(i >= steps)
        def _():
            k = i - steps
            gacc[...] += nn(down_out[:, pl.ds(pl.multiple_of(k * eb, eb), eb)], e_ref[...])

        @pl.when(i == steps + esteps - 1)
        def _():
            for q in range(width // fold):
                grad_out[:, q * feats:(q + 1) * feats] = gacc[:, q * fold:(q + 1) * fold].T.astype(BF)
            grad_out[:, width // fold * feats:] = p_ref[...]

    return pl.pallas_call(
        body,
        out_shape=(
            jax.ShapeDtypeStruct((feats, n_edges), BF),
            jax.ShapeDtypeStruct((fold, lanes), BF),
        ),
        grid=(steps + esteps,),
        in_specs=[
            pl.BlockSpec((per, feats, slot), lambda i: (jnp.minimum(i, steps - 1), 0, 0)),
            pl.BlockSpec((1, per * slot), lambda i: (0, jnp.minimum(i, steps - 1))),
            pl.BlockSpec((eb, width), lambda i: (jnp.maximum(i - steps, 0), 0)),
            full(piece.shape),
        ],
        out_specs=(full((feats, n_edges)), full((fold, lanes))),
        scratch_shapes=[
            pltpu.VMEM((eblocks * feats, LO), F32),
            pltpu.VMEM((eblocks * feats, per * slot), BF),
            pltpu.VMEM((LO, per * slot), BF),
            pltpu.VMEM((feats, width), F32),
        ],
        compiler_params=params(),
        name="returned",
    )(ret, send_idx, edges, piece)


def edges_kernel(g_down_t, w_down_t):
    feats, n_edges = g_down_t.shape
    width = w_down_t.shape[1]
    eb = 1024

    def body(g_ref, w_ref, out_ref):
        out_ref[...] = tn(g_ref[...], w_ref[...]).astype(BF)

    return pl.pallas_call(
        body,
        out_shape=jax.ShapeDtypeStruct((n_edges, width), BF),
        grid=(n_edges // eb,),
        in_specs=[pl.BlockSpec((feats, eb), lambda i: (0, i)), full(w_down_t.shape)],
        out_specs=pl.BlockSpec((eb, width), lambda i: (i, 0)),
        compiler_params=params(),
        name="grad_edges",
    )(g_down_t, w_down_t)


def exchange(x, axes):
    return lax.all_to_all(x, axes, split_axis=0, concat_axis=0, tiled=True)


def total_kernel(got, n_dp, feats, own):
    n, pair, lanes = got.shape
    share = feats // n_dp
    groups = (lanes - own) // feats * 3
    out_lanes = own + groups * feats

    def body(x_ref, out_ref):
        sums = jnp.sum(x_ref[...].astype(F32).reshape(n_dp, n // n_dp, pair, lanes), axis=1)
        parts = [jnp.sum(sums[:, :, :own], axis=0)]
        where = lax.broadcasted_iota(jnp.int32, (n_dp, pair, feats), 2) // share
        mine = where == lax.broadcasted_iota(jnp.int32, (n_dp, pair, feats), 0)
        for q in range(groups):
            piece = sums[:, :, own + q * share:own + (q + 1) * share]
            wide = jnp.concatenate([piece] * n_dp, axis=2)
            parts.append(jnp.sum(jnp.where(mine, wide, 0.0), axis=0))
        row = jnp.concatenate(parts, axis=1).astype(BF)
        out_ref[...] = jnp.broadcast_to(row[None], out_ref.shape)

    return pl.pallas_call(
        body,
        out_shape=jax.ShapeDtypeStruct((n, pair, out_lanes), BF),
        compiler_params=params(),
        name="totals",
    )(got)


def scatter_dp(x, n_dp):
    d = lax.axis_index("dp")
    for bit in reversed(range(n_dp.bit_length() - 1)):
        half = x.shape[0] // 2
        b = (d >> bit) & 1
        keep = lax.dynamic_slice_in_dim(x, b * half, half, 0)
        give = lax.dynamic_slice_in_dim(x, (1 - b) * half, half, 0)
        x = keep + lax.ppermute(give, "dp", [(k, k ^ (1 << bit)) for k in range(n_dp)])
    return x


def share_out(part, fold):
    share, cols = part.shape
    tall = jnp.pad(part.T.astype(BF), ((0, -cols % fold), (0, 0)))
    wide = jnp.concatenate([tall[k:k + fold] for k in range(0, tall.shape[0], fold)], axis=1)
    return jnp.pad(wide, ((0, 0), (0, -wide.shape[1] % 128)))


def reduce_all(slab, n_dp, n_graph, feats, own):
    n = n_dp * n_graph
    axes = ("dp", "graph")
    got = exchange(slab.reshape(n, slab.shape[0] // n, slab.shape[1]), axes)
    sent = total_kernel(got, n_dp, feats, own)
    return exchange(sent, axes).reshape(slab.shape[0], sent.shape[2])


def make_shards(n_dp, n_graph):
    def shards(edges, send_rows, trip_src, trip_dst, basis_values, cotangent, w_down, w_up, w_basis):
        edge_rows = edges[0]
        basis = basis_values[0]
        n_edges, width = edge_rows.shape
        feats = w_down.shape[1]
        nb = basis.shape[0]
        sent = send_kernel(edge_rows, w_down, send_rows, n_graph)
        received = exchange(sent, "graph")
        src, sent_now = lax.optimization_barrier((trip_src, sent))
        trip, ranges = sort_kernel(src, trip_dst, basis, n_graph)
        w_basis_t = jnp.pad(w_basis.T, ((0, 0), (0, trip.shape[1] - nb)))
        src_t, agg_t = forward_kernel(received, ranges, trip, w_basis_t, n_edges, nb)
        g_pre, g_agg_t = dense_kernel(agg_t, w_up, cotangent[0])
        g_received, g_basis = backward_kernel(
            g_agg_t, src_t, ranges, trip, w_basis_t, n_graph, nb
        )
        returned = exchange(g_received, "graph")
        n = n_dp * n_graph
        fold = 2 * n
        small = weights_kernel(agg_t, g_pre, g_basis, trip, n)
        part = scatter_dp(small, n_dp)
        returned, piece = lax.optimization_barrier((returned, share_out(part, fold)))
        g_down_t, slab = return_kernel(returned, send_rows, edge_rows, piece)
        reduced = reduce_all(slab, n_dp, n_graph, feats, width // fold * feats)
        grad_edges = edges_kernel(g_down_t, w_down.T)
        parts = [reduced[:, k * feats:(k + 1) * feats] for k in range(reduced.shape[1] // feats)]
        per = width // fold
        grad_down = jnp.concatenate(parts[:per]).astype(F32)
        grad_up = jnp.concatenate(parts[per:2 * per]).astype(F32).T
        grad_basis = parts[2 * per][:nb].astype(F32)
        return grad_edges[None], grad_down, grad_up, grad_basis

    return shards


def solution(mesh):
    shape = dict(mesh.shape)
    in_specs = (
        P("dp", "graph", None),
        P("dp", "graph"),
        P("dp", "graph"),
        P("dp", "graph"),
        P("dp", None, "graph"),
        P("dp", "graph", None),
        P(),
        P(),
        P(),
    )
    out_specs = (P("dp", "graph", None), P(), P(), P())
    return jax.shard_map(
        make_shards(shape["dp"], shape["graph"]),
        mesh=mesh,
        in_specs=in_specs,
        out_specs=out_specs,
        check_vma=False,
    )
```

```python
import jax
import jax.numpy as jnp
from jax import lax
from jax.experimental import pallas as pl
from jax.experimental.pallas import tpu as pltpu
from jax.sharding import PartitionSpec as P

LO = 256
BF = jnp.bfloat16
F32 = jnp.float32


def split(idx):
    return idx & (LO - 1), idx >> 8


def onehot(lo, width):
    rows = lax.broadcasted_iota(jnp.int32, (LO, width), 0)
    return jnp.where(rows == lo, 1.0, 0.0).astype(BF)


def nn(a, b):
    return jnp.dot(a, b, preferred_element_type=F32)


def nt(a, b):
    return lax.dot_general(a, b, (((1,), (1,)), ((), ())), preferred_element_type=F32)


def tn(a, b):
    return lax.dot_general(a, b, (((0,), (0,)), ((), ())), preferred_element_type=F32)


def pick(res, hi, blocks, feats, base=0):
    acc = jnp.zeros((feats, res.shape[1]), F32)
    for j in range(blocks):
        acc = jnp.where(hi == base + j, res[j * feats:(j + 1) * feats], acc)
    return acc


def params():
    return pltpu.CompilerParams(vmem_limit_bytes=56 * 1024 * 1024)


def full(shape):
    return pl.BlockSpec(shape, lambda i: (0,) * len(shape))


def send_kernel(edges, w_down, send_idx, peers):
    n_edges, width = edges.shape
    feats = w_down.shape[1]
    eb = 1024
    nd = n_edges // eb
    per = 16
    ng = peers // per
    slot = send_idx.shape[1] // peers
    blocks = n_edges // LO

    def body(e_ref, w_ref, i_ref, out_ref, table):
        i = pl.program_id(0)

        @pl.when(i < nd)
        def _():
            d = nn(e_ref[...], w_ref[...]).astype(BF).T
            for k in range(eb // LO):
                table[i * (eb // LO) + k] = d[:, k * LO:(k + 1) * LO]

        @pl.when(i >= nd)
        def _():
            tab = table[...].reshape(blocks * feats, LO)
            for a in range(per):
                lo, hi = split(i_ref[:, a * slot:(a + 1) * slot])
                res = nn(tab, onehot(lo, slot))
                out_ref[a] = pick(res, hi, blocks, feats).astype(BF)

    return pl.pallas_call(
        body,
        out_shape=jax.ShapeDtypeStruct((peers, feats, slot), BF),
        grid=(nd + ng,),
        in_specs=[
            pl.BlockSpec((eb, width), lambda i: (jnp.minimum(i, nd - 1), 0)),
            full(w_down.shape),
            pl.BlockSpec((1, per * slot), lambda i: (0, jnp.maximum(i - nd, 0))),
        ],
        out_specs=pl.BlockSpec((per, feats, slot), lambda i: (jnp.maximum(i - nd, 0), 0, 0)),
        scratch_shapes=[pltpu.VMEM((blocks, feats, LO), BF)],
        compiler_params=params(),
        name="send",
    )(edges, w_down, send_idx)


def sort_kernel(src, dst, basis, peers):
    trips = src.shape[1]
    nb = basis.shape[0]
    rows = -(-(nb + 4) // 16) * 16
    chunks = trips // LO
    tc = 1024
    steps = trips // tc

    def body(s_ref, d_ref, b_ref, x_out, range_out, oh_hi, first, pm, oh, acc):
        i = pl.program_id(0)

        @pl.when(i == 0)
        def _():
            acc[...] = jnp.zeros_like(acc)
            bucket = lax.broadcasted_iota(jnp.int32, (peers, trips), 0)
            hot = jnp.where(bucket == (s_ref[...] >> 8), 1.0, 0.0)
            oh_hi[...] = hot.astype(BF)
            total = jnp.broadcast_to(jnp.sum(hot, axis=1, keepdims=True), (peers, 128))
            high = jnp.floor(total * (1.0 / 256.0))
            low = total - high * 256.0
            r = lax.broadcasted_iota(jnp.int32, (peers, peers), 0)
            c = lax.broadcasted_iota(jnp.int32, (peers, peers), 1)
            before = jnp.where(c < r, 1.0, 0.0).astype(BF)
            start = 256.0 * nn(before, high.astype(BF)) + nn(before, low.astype(BF))
            first[...] = start
            edge = 256.0 * lax.broadcasted_iota(jnp.int32, (peers, 128), 1).astype(F32)
            b0 = jnp.sum(jnp.where(start + total <= edge, 1.0, 0.0), axis=0, keepdims=True)
            b1 = jnp.sum(jnp.where(start < edge + 256.0, 1.0, 0.0), axis=0, keepdims=True) - 1.0
            range_out[0:1] = jnp.minimum(b0, peers - 1.0).astype(jnp.int32)
            range_out[1:2] = b1.astype(jnp.int32)

        r = lax.broadcasted_iota(jnp.int32, (LO, LO), 0)
        c = lax.broadcasted_iota(jnp.int32, (LO, LO), 1)
        upto = jnp.where(r <= c, 1.0, 0.0).astype(BF)
        for a in range(tc // LO):
            cols = slice(a * LO, (a + 1) * LO)
            at = pl.multiple_of(i * tc + a * LO, LO)
            hot = oh_hi[:, pl.ds(at, LO)]
            count = nn(hot, upto)
            place = first[:, 0:1] + count - 1.0
            hot32 = hot.astype(F32)
            pos = jnp.sum(hot32 * place, axis=0, keepdims=True).astype(jnp.int32)
            first[...] += jnp.broadcast_to(count[:, LO - 1:LO], first.shape)
            s_lo, s_hi = split(s_ref[:, pl.ds(at, LO)])
            d_lo, d_hi = split(d_ref[:, cols])
            row = lax.broadcasted_iota(jnp.int32, (rows - nb, LO), 0)
            extra = jnp.where(row == 0, s_lo, jnp.where(row == 1, s_hi, jnp.where(row == 2, d_lo, jnp.where(row == 3, d_hi, 0))))
            x = jnp.concatenate([b_ref[:, cols].astype(F32), extra.astype(F32)], axis=0)
            lo, hi = split(pos)
            for j in range(chunks):
                pm[j * rows:(j + 1) * rows, cols] = jnp.where(hi == j, x, 0.0).astype(BF)
            oh[:, cols] = onehot(lo, LO)
        acc[...] += nt(pm[...], oh[...])

        @pl.when(i == steps - 1)
        def _():
            x_out[...] = acc[...].reshape(x_out.shape)

    return pl.pallas_call(
        body,
        out_shape=(
            jax.ShapeDtypeStruct((chunks, rows, LO), F32),
            jax.ShapeDtypeStruct((2, 128), jnp.int32),
        ),
        grid=(steps,),
        in_specs=[
            full(src.shape),
            pl.BlockSpec((1, tc), lambda i: (0, i)),
            pl.BlockSpec((nb, tc), lambda i: (0, i)),
        ],
        out_specs=(full((chunks, rows, LO)), full((2, 128))),
        scratch_shapes=[
            pltpu.VMEM((peers, trips), BF),
            pltpu.VMEM((peers, 128), F32),
            pltpu.VMEM((chunks * rows, tc), BF),
            pltpu.VMEM((LO, tc), BF),
            pltpu.VMEM((chunks * rows, LO), F32),
        ],
        compiler_params=params(),
        name="order",
    )(src, dst, basis)


NEAR = 3


def forward_kernel(recv, ranges, trip, w_basis_t, n_edges, nb):
    peers, feats, _ = recv.shape
    chunks, rows, _ = trip.shape
    per = 16
    steps = chunks // per
    eblocks = n_edges // LO

    def body(rg, r_ref, x_ref, w_ref, src_out, agg_out, acc, pm, oh, source):
        i = pl.program_id(0)

        @pl.when(i == 0)
        def _():
            acc[...] = jnp.zeros_like(acc)

        def ids(a, k):
            return x_ref[a, nb + k:nb + k + 1].astype(jnp.int32)

        far = jnp.int32(0)
        for a in range(per):
            b0 = rg[0, i * per + a]
            far = jnp.maximum(far, rg[1, i * per + a] - b0)
            hot = onehot(ids(a, 0), LO)
            hi = ids(a, 1)
            at = jnp.minimum(b0, peers - NEAR)
            near = r_ref[pl.ds(at, NEAR)].reshape(NEAR * feats, LO)
            source[a] = pick(nn(near, hot), hi, NEAR, feats, at)

        @pl.when(far >= NEAR)
        def _():
            for a in range(per):
                def more(b, _, a=a):
                    res = nn(r_ref[b], onehot(ids(a, 0), LO))
                    source[a] = jnp.where(ids(a, 1) == b, res, source[a])
                    return 0
                lax.fori_loop(rg[0, i * per + a] + NEAR, rg[1, i * per + a] + 1, more, 0)

        for a in range(per):
            cols = slice(a * LO, (a + 1) * LO)
            src_out[a] = source[a].astype(BF)
            product = source[a] * nn(w_ref[...], x_ref[a].astype(BF))
            hi = ids(a, 3)
            for j in range(eblocks):
                pm[j * feats:(j + 1) * feats, cols] = jnp.where(hi == j, product, 0.0).astype(BF)
            oh[:, cols] = onehot(ids(a, 2), LO)
        acc[...] += nt(pm[...], oh[...])

        @pl.when(i == steps - 1)
        def _():
            for j in range(eblocks):
                agg_out[:, j * LO:(j + 1) * LO] = acc[j * feats:(j + 1) * feats].astype(BF)

    def whole(shape):
        return pl.BlockSpec(shape, lambda i, rg: (0,) * len(shape))

    return pl.pallas_call(
        body,
        out_shape=(
            jax.ShapeDtypeStruct((chunks, feats, LO), BF),
            jax.ShapeDtypeStruct((feats, n_edges), BF),
        ),
        grid_spec=pltpu.PrefetchScalarGridSpec(
            num_scalar_prefetch=1,
            grid=(steps,),
            in_specs=[
                pl.BlockSpec(memory_space=pltpu.VMEM),
                pl.BlockSpec((per, rows, LO), lambda i, rg: (i, 0, 0)),
                whole(w_basis_t.shape),
            ],
            out_specs=(
                pl.BlockSpec((per, feats, LO), lambda i, rg: (i, 0, 0)),
                whole((feats, n_edges)),
            ),
            scratch_shapes=[
                pltpu.VMEM((eblocks * feats, LO), F32),
                pltpu.VMEM((eblocks * feats, per * LO), BF),
                pltpu.VMEM((LO, per * LO), BF),
                pltpu.VMEM((per, feats, LO), F32),
            ],
        ),
        compiler_params=params(),
        name="forward",
    )(ranges, recv, trip, w_basis_t)


def dense_kernel(agg_t, w_up, cot):
    feats, n_edges = agg_t.shape
    width = w_up.shape[1]
    eb = 1024
    steps = n_edges // eb

    def body(a_ref, w_ref, c_ref, p_out, g_out):
        for k in range(eb // 256):
            r = slice(k * 256, (k + 1) * 256)
            pre = tn(a_ref[:, r], w_ref[...])
            t = 0.5 * jnp.tanh(0.5 * pre)
            g_pre = (c_ref[r].astype(F32) * (0.5 + t) * (1.0 + pre * (0.5 - t))).astype(BF)
            p_out[r] = g_pre
            g_out[:, r] = nt(w_ref[...], g_pre).astype(BF)

    return pl.pallas_call(
        body,
        out_shape=(
            jax.ShapeDtypeStruct((n_edges, width), BF),
            jax.ShapeDtypeStruct((feats, n_edges), BF),
        ),
        grid=(steps,),
        in_specs=[
            pl.BlockSpec((feats, eb), lambda i: (0, i)),
            full(w_up.shape),
            pl.BlockSpec((eb, width), lambda i: (i, 0)),
        ],
        out_specs=(
            pl.BlockSpec((eb, width), lambda i: (i, 0)),
            pl.BlockSpec((feats, eb), lambda i: (0, i)),
        ),
        compiler_params=params(),
        name="dense",
    )(agg_t, w_up, cot)


def backward_kernel(g_agg_t, src_t, ranges, trip, w_basis_t, peers, nb):
    feats, n_edges = g_agg_t.shape
    chunks, rows, _ = trip.shape
    per = 8
    steps = chunks // per
    eblocks = n_edges // LO

    def body(rg, g_ref, st_ref, x_ref, w_ref, out_ref, gb_out, table, acc, source):
        i = pl.program_id(0)

        @pl.when(i == 0)
        def _():
            acc[...] = jnp.zeros_like(acc)
            for j in range(eblocks):
                table[j * feats:(j + 1) * feats] = g_ref[:, j * LO:(j + 1) * LO]

        def ids(a, k):
            return x_ref[a, nb + k:nb + k + 1].astype(jnp.int32)

        far = jnp.int32(0)
        for a in range(per):
            g_trip = pick(nn(table[...], onehot(ids(a, 2), LO)), ids(a, 3), eblocks, feats)
            gb_out[a] = g_trip * st_ref[a].astype(F32)
            source[a] = g_trip * nn(w_ref[...], x_ref[a].astype(BF))
        for a in range(per):
            b0 = rg[0, i * per + a]
            far = jnp.maximum(far, rg[1, i * per + a] - b0)
            hot = onehot(ids(a, 0), LO)
            hi = ids(a, 1)
            at = jnp.minimum(b0, peers - NEAR)
            near = jnp.concatenate([jnp.where(hi == at + n, source[a], 0.0) for n in range(NEAR)]).astype(BF)
            acc[pl.ds(at, NEAR)] += nt(near, hot).reshape(NEAR, feats, LO)

        @pl.when(far >= NEAR)
        def _():
            for a in range(per):
                def more(b, _, a=a):
                    part = jnp.where(ids(a, 1) == b, source[a], 0.0).astype(BF)
                    acc[b] += nt(part, onehot(ids(a, 0), LO))
                    return 0
                lax.fori_loop(rg[0, i * per + a] + NEAR, rg[1, i * per + a] + 1, more, 0)

        @pl.when(i == steps - 1)
        def _():
            out_ref[...] = acc[...].astype(BF)

    def whole(shape):
        return pl.BlockSpec(shape, lambda i, rg: (0,) * len(shape))

    return pl.pallas_call(
        body,
        out_shape=(
            jax.ShapeDtypeStruct((peers, feats, LO), BF),
            jax.ShapeDtypeStruct((chunks, feats, LO), F32),
        ),
        grid_spec=pltpu.PrefetchScalarGridSpec(
            num_scalar_prefetch=1,
            grid=(steps,),
            in_specs=[
                whole(g_agg_t.shape),
                pl.BlockSpec((per, feats, LO), lambda i, rg: (i, 0, 0)),
                pl.BlockSpec((per, rows, LO), lambda i, rg: (i, 0, 0)),
                whole(w_basis_t.shape),
            ],
            out_specs=(
                whole((peers, feats, LO)),
                pl.BlockSpec((per, feats, LO), lambda i, rg: (i, 0, 0)),
            ),
            scratch_shapes=[
                pltpu.VMEM((eblocks * feats, LO), BF),
                pltpu.VMEM((peers, feats, LO), F32),
                pltpu.VMEM((per, feats, LO), F32),
            ],
        ),
        compiler_params=params(),
        name="backward",
    )(ranges, g_agg_t, src_t, trip, w_basis_t)


def weights_kernel(agg_t, g_pre, g_basis, trip, lines):
    feats, n_edges = agg_t.shape
    width = g_pre.shape[1]
    chunks, rows, _ = trip.shape
    steps = 4
    eb = n_edges // steps
    per = chunks // steps

    def body(a_ref, p_ref, g_ref, x_ref, out_ref, up, bt):
        i = pl.program_id(0)

        @pl.when(i == 0)
        def _():
            up[...] = jnp.zeros_like(up)
            bt[...] = jnp.zeros_like(bt)

        up[...] += nn(a_ref[...], p_ref[...])
        for a in range(per):
            top = g_ref[a].astype(BF)
            low = (g_ref[a] - top.astype(F32)).astype(BF)
            basis = x_ref[a].astype(BF)
            bt[...] += nt(basis, top) + nt(basis, low)

        @pl.when(i == steps - 1)
        def _():
            out_ref[:, :width] = up[...]
            tall = jnp.concatenate([bt[...], jnp.zeros((lines - rows, feats), F32)])
            out_ref[:, width:] = tall.T

    return pl.pallas_call(
        body,
        out_shape=jax.ShapeDtypeStruct((feats, width + lines), F32),
        grid=(steps,),
        in_specs=[
            pl.BlockSpec((feats, eb), lambda i: (0, i)),
            pl.BlockSpec((eb, width), lambda i: (i, 0)),
            pl.BlockSpec((per, feats, LO), lambda i: (i, 0, 0)),
            pl.BlockSpec((per, rows, LO), lambda i: (i, 0, 0)),
        ],
        out_specs=full((feats, width + lines)),
        scratch_shapes=[pltpu.VMEM((feats, width), F32), pltpu.VMEM((rows, feats), F32)],
        compiler_params=params(),
        name="weights",
    )(agg_t, g_pre, g_basis, trip)


def return_kernel(ret, send_idx, edges, piece):
    peers, feats, slot = ret.shape
    n_edges, width = edges.shape
    fold = piece.shape[0]
    lanes = width // fold * feats + piece.shape[1]
    per = 32
    steps = peers // per
    eblocks = n_edges // LO
    eb = 2048
    esteps = n_edges // eb

    def body(r_ref, i_ref, e_ref, p_ref, down_out, grad_out, acc, pm, oh, gacc):
        i = pl.program_id(0)

        @pl.when(i == 0)
        def _():
            acc[...] = jnp.zeros_like(acc)
            gacc[...] = jnp.zeros_like(gacc)

        @pl.when(i < steps)
        def _():
            for a in range(per):
                cols = slice(a * slot, (a + 1) * slot)
                lo, hi = split(i_ref[:, cols])
                rows = r_ref[i * per + a].astype(F32)
                for j in range(eblocks):
                    pm[j * feats:(j + 1) * feats, cols] = jnp.where(hi == j, rows, 0.0).astype(BF)
                oh[:, cols] = onehot(lo, slot)
            acc[...] += nt(pm[...], oh[...])

        @pl.when(i == steps - 1)
        def _():
            for j in range(eblocks):
                down_out[:, j * LO:(j + 1) * LO] = acc[j * feats:(j + 1) * feats].astype(BF)

        @pl.when(i >= steps)
        def _():
            k = i - steps
            gacc[...] += nn(down_out[:, pl.ds(pl.multiple_of(k * eb, eb), eb)], e_ref[...])

        @pl.when(i == steps + esteps - 1)
        def _():
            for q in range(width // fold):
                grad_out[:, q * feats:(q + 1) * feats] = gacc[:, q * fold:(q + 1) * fold].T.astype(BF)
            grad_out[:, width // fold * feats:] = p_ref[...]

    return pl.pallas_call(
        body,
        out_shape=(
            jax.ShapeDtypeStruct((feats, n_edges), BF),
            jax.ShapeDtypeStruct((fold, lanes), BF),
        ),
        grid=(steps + esteps,),
        in_specs=[
            pl.BlockSpec(memory_space=pltpu.VMEM),
            pl.BlockSpec((1, per * slot), lambda i: (0, jnp.minimum(i, steps - 1))),
            pl.BlockSpec((eb, width), lambda i: (jnp.maximum(i - steps, 0), 0)),
            full(piece.shape),
        ],
        out_specs=(full((feats, n_edges)), full((fold, lanes))),
        scratch_shapes=[
            pltpu.VMEM((eblocks * feats, LO), F32),
            pltpu.VMEM((eblocks * feats, per * slot), BF),
            pltpu.VMEM((LO, per * slot), BF),
            pltpu.VMEM((feats, width), F32),
        ],
        compiler_params=params(),
        name="returned",
    )(ret, send_idx, edges, piece)


def edges_kernel(g_down_t, w_down_t):
    feats, n_edges = g_down_t.shape
    width = w_down_t.shape[1]
    eb = 1024

    def body(g_ref, w_ref, out_ref):
        out_ref[...] = tn(g_ref[...], w_ref[...]).astype(BF)

    return pl.pallas_call(
        body,
        out_shape=jax.ShapeDtypeStruct((n_edges, width), BF),
        grid=(n_edges // eb,),
        in_specs=[pl.BlockSpec((feats, eb), lambda i: (0, i)), full(w_down_t.shape)],
        out_specs=pl.BlockSpec((eb, width), lambda i: (i, 0)),
        compiler_params=params(),
        name="grad_edges",
    )(g_down_t, w_down_t)


def exchange(x, axes):
    return lax.all_to_all(x, axes, split_axis=0, concat_axis=0, tiled=True)


def total_kernel(got, n_dp, feats, own):
    n, pair, lanes = got.shape
    share = feats // n_dp
    groups = (lanes - own) // feats * 3
    out_lanes = own + groups * feats

    def body(x_ref, out_ref):
        sums = jnp.sum(x_ref[...].astype(F32).reshape(n_dp, n // n_dp, pair, lanes), axis=1)
        parts = [jnp.sum(sums[:, :, :own], axis=0)]
        where = lax.broadcasted_iota(jnp.int32, (n_dp, pair, feats), 2) // share
        mine = where == lax.broadcasted_iota(jnp.int32, (n_dp, pair, feats), 0)
        for q in range(groups):
            piece = sums[:, :, own + q * share:own + (q + 1) * share]
            wide = jnp.concatenate([piece] * n_dp, axis=2)
            parts.append(jnp.sum(jnp.where(mine, wide, 0.0), axis=0))
        row = jnp.concatenate(parts, axis=1).astype(BF)
        out_ref[...] = jnp.broadcast_to(row[None], out_ref.shape)

    return pl.pallas_call(
        body,
        out_shape=jax.ShapeDtypeStruct((n, pair, out_lanes), BF),
        compiler_params=params(),
        name="totals",
    )(got)


def scatter_dp(x, n_dp):
    d = lax.axis_index("dp")
    for bit in reversed(range(n_dp.bit_length() - 1)):
        half = x.shape[0] // 2
        b = (d >> bit) & 1
        keep = lax.dynamic_slice_in_dim(x, b * half, half, 0)
        give = lax.dynamic_slice_in_dim(x, (1 - b) * half, half, 0)
        x = keep + lax.ppermute(give, "dp", [(k, k ^ (1 << bit)) for k in range(n_dp)])
    return x


def share_out(part, fold):
    share, cols = part.shape
    tall = jnp.pad(part.T.astype(BF), ((0, -cols % fold), (0, 0)))
    wide = jnp.concatenate([tall[k:k + fold] for k in range(0, tall.shape[0], fold)], axis=1)
    return jnp.pad(wide, ((0, 0), (0, -wide.shape[1] % 128)))


def reduce_all(slab, n_dp, n_graph, feats, own):
    n = n_dp * n_graph
    axes = ("dp", "graph")
    got = exchange(slab.reshape(n, slab.shape[0] // n, slab.shape[1]), axes)
    sent = total_kernel(got, n_dp, feats, own)
    return exchange(sent, axes).reshape(slab.shape[0], sent.shape[2])


def make_shards(n_dp, n_graph):
    def shards(edges, send_rows, trip_src, trip_dst, basis_values, cotangent, w_down, w_up, w_basis):
        edge_rows = edges[0]
        basis = basis_values[0]
        n_edges, width = edge_rows.shape
        feats = w_down.shape[1]
        nb = basis.shape[0]
        sent = send_kernel(edge_rows, w_down, send_rows, n_graph)
        received = pltpu.with_memory_space_constraint(exchange(sent, "graph"), pltpu.VMEM)
        src, sent_now = lax.optimization_barrier((trip_src, sent))
        trip, ranges = sort_kernel(src, trip_dst, basis, n_graph)
        w_basis_t = jnp.pad(w_basis.T, ((0, 0), (0, trip.shape[1] - nb)))
        src_t, agg_t = forward_kernel(received, ranges, trip, w_basis_t, n_edges, nb)
        g_pre, g_agg_t = dense_kernel(agg_t, w_up, cotangent[0])
        g_received, g_basis = backward_kernel(
            g_agg_t, src_t, ranges, trip, w_basis_t, n_graph, nb
        )
        returned = exchange(g_received, "graph")
        n = n_dp * n_graph
        fold = 2 * n
        small = weights_kernel(agg_t, g_pre, g_basis, trip, n)
        part = scatter_dp(small, n_dp)
        returned, piece = lax.optimization_barrier((returned, share_out(part, fold)))
        returned = pltpu.with_memory_space_constraint(returned, pltpu.VMEM)
        g_down_t, slab = return_kernel(returned, send_rows, edge_rows, piece)
        reduced = reduce_all(slab, n_dp, n_graph, feats, width // fold * feats)
        grad_edges = edges_kernel(g_down_t, w_down.T)
        parts = [reduced[:, k * feats:(k + 1) * feats] for k in range(reduced.shape[1] // feats)]
        per = width // fold
        grad_down = jnp.concatenate(parts[:per]).astype(F32)
        grad_up = jnp.concatenate(parts[per:2 * per]).astype(F32).T
        grad_basis = parts[2 * per][:nb].astype(F32)
        return grad_edges[None], grad_down, grad_up, grad_basis

    return shards


def solution(mesh):
    shape = dict(mesh.shape)
    in_specs = (
        P("dp", "graph", None),
        P("dp", "graph"),
        P("dp", "graph"),
        P("dp", "graph"),
        P("dp", None, "graph"),
        P("dp", "graph", None),
        P(),
        P(),
        P(),
    )
    out_specs = (P("dp", "graph", None), P(), P(), P())
    return jax.shard_map(
        make_shards(shape["dp"], shape["graph"]),
        mesh=mesh,
        in_specs=in_specs,
        out_specs=out_specs,
        check_vma=False,
    )
```

```python
import jax
import jax.numpy as jnp
from jax import lax
from jax.experimental import pallas as pl
from jax.experimental.pallas import tpu as pltpu
from jax.sharding import PartitionSpec as P

LO = 256
BF = jnp.bfloat16
F32 = jnp.float32


def split(idx):
    return idx & (LO - 1), idx >> 8


def onehot(lo, width):
    rows = lax.broadcasted_iota(jnp.int32, (LO, width), 0)
    return jnp.where(rows == lo, 1.0, 0.0).astype(BF)


def nn(a, b):
    return jnp.dot(a, b, preferred_element_type=F32)


def nt(a, b):
    return lax.dot_general(a, b, (((1,), (1,)), ((), ())), preferred_element_type=F32)


def tn(a, b):
    return lax.dot_general(a, b, (((0,), (0,)), ((), ())), preferred_element_type=F32)


def pick(res, hi, blocks, feats, base=0):
    acc = jnp.zeros((feats, res.shape[1]), F32)
    for j in range(blocks):
        acc = jnp.where(hi == base + j, res[j * feats:(j + 1) * feats], acc)
    return acc


def params():
    return pltpu.CompilerParams(vmem_limit_bytes=56 * 1024 * 1024)


def full(shape):
    return pl.BlockSpec(shape, lambda i: (0,) * len(shape))


def send_kernel(edges, w_down, send_idx, peers):
    n_edges, width = edges.shape
    feats = w_down.shape[1]
    eb = 1024
    nd = n_edges // eb
    per = 16
    ng = peers // per
    slot = send_idx.shape[1] // peers
    blocks = n_edges // LO

    def body(e_ref, w_ref, i_ref, out_ref, table):
        i = pl.program_id(0)

        @pl.when(i < nd)
        def _():
            d = nn(e_ref[...], w_ref[...]).astype(BF).T
            for k in range(eb // LO):
                table[i * (eb // LO) + k] = d[:, k * LO:(k + 1) * LO]

        @pl.when(i >= nd)
        def _():
            tab = table[...].reshape(blocks * feats, LO)
            for a in range(per):
                lo, hi = split(i_ref[:, a * slot:(a + 1) * slot])
                res = nn(tab, onehot(lo, slot))
                out_ref[a] = pick(res, hi, blocks, feats).astype(BF)

    return pl.pallas_call(
        body,
        out_shape=jax.ShapeDtypeStruct((peers, feats, slot), BF),
        grid=(nd + ng,),
        in_specs=[
            pl.BlockSpec((eb, width), lambda i: (jnp.minimum(i, nd - 1), 0)),
            full(w_down.shape),
            pl.BlockSpec((1, per * slot), lambda i: (0, jnp.maximum(i - nd, 0))),
        ],
        out_specs=pl.BlockSpec((per, feats, slot), lambda i: (jnp.maximum(i - nd, 0), 0, 0)),
        scratch_shapes=[pltpu.VMEM((blocks, feats, LO), BF)],
        compiler_params=params(),
        name="send",
    )(edges, w_down, send_idx)


def sort_kernel(src, dst, basis, peers):
    trips = src.shape[1]
    nb = basis.shape[0]
    rows = -(-(nb + 4) // 16) * 16
    chunks = trips // LO
    tc = 1024
    steps = trips // tc

    def body(s_ref, d_ref, b_ref, x_out, range_out, oh_hi, first, pm, oh, acc):
        i = pl.program_id(0)

        @pl.when(i == 0)
        def _():
            acc[...] = jnp.zeros_like(acc)
            bucket = lax.broadcasted_iota(jnp.int32, (peers, trips), 0)
            hot = jnp.where(bucket == (s_ref[...] >> 8), 1.0, 0.0)
            oh_hi[...] = hot.astype(BF)
            total = jnp.broadcast_to(jnp.sum(hot, axis=1, keepdims=True), (peers, 128))
            high = jnp.floor(total * (1.0 / 256.0))
            low = total - high * 256.0
            r = lax.broadcasted_iota(jnp.int32, (peers, peers), 0)
            c = lax.broadcasted_iota(jnp.int32, (peers, peers), 1)
            before = jnp.where(c < r, 1.0, 0.0).astype(BF)
            start = 256.0 * nn(before, high.astype(BF)) + nn(before, low.astype(BF))
            first[...] = start
            edge = 256.0 * lax.broadcasted_iota(jnp.int32, (peers, 128), 1).astype(F32)
            b0 = jnp.sum(jnp.where(start + total <= edge, 1.0, 0.0), axis=0, keepdims=True)
            b1 = jnp.sum(jnp.where(start < edge + 256.0, 1.0, 0.0), axis=0, keepdims=True) - 1.0
            range_out[0:1] = jnp.minimum(b0, peers - 1.0).astype(jnp.int32)
            range_out[1:2] = b1.astype(jnp.int32)

        r = lax.broadcasted_iota(jnp.int32, (LO, LO), 0)
        c = lax.broadcasted_iota(jnp.int32, (LO, LO), 1)
        upto = jnp.where(r <= c, 1.0, 0.0).astype(BF)
        for a in range(tc // LO):
            cols = slice(a * LO, (a + 1) * LO)
            at = pl.multiple_of(i * tc + a * LO, LO)
            hot = oh_hi[:, pl.ds(at, LO)]
            count = nn(hot, upto)
            place = first[:, 0:1] + count - 1.0
            hot32 = hot.astype(F32)
            pos = jnp.sum(hot32 * place, axis=0, keepdims=True).astype(jnp.int32)
            first[...] += jnp.broadcast_to(count[:, LO - 1:LO], first.shape)
            s_lo, s_hi = split(s_ref[:, pl.ds(at, LO)])
            d_lo, d_hi = split(d_ref[:, cols])
            row = lax.broadcasted_iota(jnp.int32, (rows - nb, LO), 0)
            extra = jnp.where(row == 0, s_lo, jnp.where(row == 1, s_hi, jnp.where(row == 2, d_lo, jnp.where(row == 3, d_hi, 0))))
            x = jnp.concatenate([b_ref[:, cols].astype(F32), extra.astype(F32)], axis=0)
            lo, hi = split(pos)
            for j in range(chunks):
                pm[j * rows:(j + 1) * rows, cols] = jnp.where(hi == j, x, 0.0).astype(BF)
            oh[:, cols] = onehot(lo, LO)
        acc[...] += nt(pm[...], oh[...])

        @pl.when(i == steps - 1)
        def _():
            x_out[...] = acc[...].reshape(x_out.shape)

    return pl.pallas_call(
        body,
        out_shape=(
            jax.ShapeDtypeStruct((chunks, rows, LO), F32),
            jax.ShapeDtypeStruct((2, 128), jnp.int32),
        ),
        grid=(steps,),
        in_specs=[
            full(src.shape),
            pl.BlockSpec((1, tc), lambda i: (0, i)),
            pl.BlockSpec((nb, tc), lambda i: (0, i)),
        ],
        out_specs=(full((chunks, rows, LO)), full((2, 128))),
        scratch_shapes=[
            pltpu.VMEM((peers, trips), BF),
            pltpu.VMEM((peers, 128), F32),
            pltpu.VMEM((chunks * rows, tc), BF),
            pltpu.VMEM((LO, tc), BF),
            pltpu.VMEM((chunks * rows, LO), F32),
        ],
        compiler_params=params(),
        name="order",
    )(src, dst, basis)


NEAR = 3


def forward_kernel(recv, ranges, trip, w_basis_t, n_edges, nb):
    peers, feats, _ = recv.shape
    chunks, rows, _ = trip.shape
    per = 16
    steps = chunks // per
    eblocks = n_edges // LO

    def body(rg, r_ref, x_ref, w_ref, src_out, agg_out, acc, pm, oh, source):
        i = pl.program_id(0)

        @pl.when(i == 0)
        def _():
            acc[...] = jnp.zeros_like(acc)

        def ids(a, k):
            return x_ref[a, nb + k:nb + k + 1].astype(jnp.int32)

        far = jnp.int32(0)
        for a in range(per):
            b0 = rg[0, i * per + a]
            far = jnp.maximum(far, rg[1, i * per + a] - b0)
            hot = onehot(ids(a, 0), LO)
            hi = ids(a, 1)
            at = jnp.minimum(b0, peers - NEAR)
            near = r_ref[pl.ds(at, NEAR)].reshape(NEAR * feats, LO)
            source[a] = pick(nn(near, hot), hi, NEAR, feats, at)

        @pl.when(far >= NEAR)
        def _():
            for a in range(per):
                def more(b, _, a=a):
                    res = nn(r_ref[b], onehot(ids(a, 0), LO))
                    source[a] = jnp.where(ids(a, 1) == b, res, source[a])
                    return 0
                lax.fori_loop(rg[0, i * per + a] + NEAR, rg[1, i * per + a] + 1, more, 0)

        for a in range(per):
            cols = slice(a * LO, (a + 1) * LO)
            src_out[a] = source[a].astype(BF)
            product = source[a] * nn(w_ref[...], x_ref[a].astype(BF))
            hi = ids(a, 3)
            for j in range(eblocks):
                pm[j * feats:(j + 1) * feats, cols] = jnp.where(hi == j, product, 0.0).astype(BF)
            oh[:, cols] = onehot(ids(a, 2), LO)
        acc[...] += nt(pm[...], oh[...])

        @pl.when(i == steps - 1)
        def _():
            for j in range(eblocks):
                agg_out[:, j * LO:(j + 1) * LO] = acc[j * feats:(j + 1) * feats].astype(BF)

    def whole(shape):
        return pl.BlockSpec(shape, lambda i, rg: (0,) * len(shape))

    return pl.pallas_call(
        body,
        out_shape=(
            jax.ShapeDtypeStruct((chunks, feats, LO), BF),
            jax.ShapeDtypeStruct((feats, n_edges), BF),
        ),
        grid_spec=pltpu.PrefetchScalarGridSpec(
            num_scalar_prefetch=1,
            grid=(steps,),
            in_specs=[
                pl.BlockSpec(memory_space=pltpu.VMEM),
                pl.BlockSpec((per, rows, LO), lambda i, rg: (i, 0, 0)),
                whole(w_basis_t.shape),
            ],
            out_specs=(
                pl.BlockSpec((per, feats, LO), lambda i, rg: (i, 0, 0)),
                whole((feats, n_edges)),
            ),
            scratch_shapes=[
                pltpu.VMEM((eblocks * feats, LO), F32),
                pltpu.VMEM((eblocks * feats, per * LO), BF),
                pltpu.VMEM((LO, per * LO), BF),
                pltpu.VMEM((per, feats, LO), F32),
            ],
        ),
        compiler_params=params(),
        name="forward",
    )(ranges, recv, trip, w_basis_t)


def dense_kernel(agg_t, w_up, cot):
    feats, n_edges = agg_t.shape
    width = w_up.shape[1]
    eb = 1024
    steps = n_edges // eb

    def body(a_ref, w_ref, c_ref, p_out, g_out):
        for k in range(eb // 256):
            r = slice(k * 256, (k + 1) * 256)
            pre = tn(a_ref[:, r], w_ref[...])
            t = 0.5 * jnp.tanh(0.5 * pre)
            g_pre = (c_ref[r].astype(F32) * (0.5 + t) * (1.0 + pre * (0.5 - t))).astype(BF)
            p_out[r] = g_pre
            g_out[:, r] = nt(w_ref[...], g_pre).astype(BF)

    return pl.pallas_call(
        body,
        out_shape=(
            jax.ShapeDtypeStruct((n_edges, width), BF),
            jax.ShapeDtypeStruct((feats, n_edges), BF),
        ),
        grid=(steps,),
        in_specs=[
            pl.BlockSpec((feats, eb), lambda i: (0, i)),
            full(w_up.shape),
            pl.BlockSpec((eb, width), lambda i: (i, 0)),
        ],
        out_specs=(
            pl.BlockSpec((eb, width), lambda i: (i, 0)),
            pl.BlockSpec((feats, eb), lambda i: (0, i)),
        ),
        compiler_params=params(),
        name="dense",
    )(agg_t, w_up, cot)


def backward_kernel(g_agg_t, src_t, ranges, trip, w_basis_t, peers, nb):
    feats, n_edges = g_agg_t.shape
    chunks, rows, _ = trip.shape
    per = 8
    steps = chunks // per
    eblocks = n_edges // LO

    def body(rg, g_ref, st_ref, x_ref, w_ref, out_ref, gb_out, table, acc, source):
        i = pl.program_id(0)

        @pl.when(i == 0)
        def _():
            acc[...] = jnp.zeros_like(acc)
            for j in range(eblocks):
                table[j * feats:(j + 1) * feats] = g_ref[:, j * LO:(j + 1) * LO]

        def ids(a, k):
            return x_ref[a, nb + k:nb + k + 1].astype(jnp.int32)

        far = jnp.int32(0)
        for a in range(per):
            g_trip = pick(nn(table[...], onehot(ids(a, 2), LO)), ids(a, 3), eblocks, feats)
            gb_out[a] = g_trip * st_ref[a].astype(F32)
            source[a] = g_trip * nn(w_ref[...], x_ref[a].astype(BF))
        for a in range(per):
            b0 = rg[0, i * per + a]
            far = jnp.maximum(far, rg[1, i * per + a] - b0)
            hot = onehot(ids(a, 0), LO)
            hi = ids(a, 1)
            at = jnp.minimum(b0, peers - NEAR)
            near = jnp.concatenate([jnp.where(hi == at + n, source[a], 0.0) for n in range(NEAR)]).astype(BF)
            acc[pl.ds(at, NEAR)] += nt(near, hot).reshape(NEAR, feats, LO)

        @pl.when(far >= NEAR)
        def _():
            for a in range(per):
                def more(b, _, a=a):
                    part = jnp.where(ids(a, 1) == b, source[a], 0.0).astype(BF)
                    acc[b] += nt(part, onehot(ids(a, 0), LO))
                    return 0
                lax.fori_loop(rg[0, i * per + a] + NEAR, rg[1, i * per + a] + 1, more, 0)

        @pl.when(i == steps - 1)
        def _():
            out_ref[...] = acc[...].astype(BF)

    def whole(shape):
        return pl.BlockSpec(shape, lambda i, rg: (0,) * len(shape))

    return pl.pallas_call(
        body,
        out_shape=(
            jax.ShapeDtypeStruct((peers, feats, LO), BF),
            jax.ShapeDtypeStruct((chunks, feats, LO), F32),
        ),
        grid_spec=pltpu.PrefetchScalarGridSpec(
            num_scalar_prefetch=1,
            grid=(steps,),
            in_specs=[
                whole(g_agg_t.shape),
                pl.BlockSpec((per, feats, LO), lambda i, rg: (i, 0, 0)),
                pl.BlockSpec((per, rows, LO), lambda i, rg: (i, 0, 0)),
                whole(w_basis_t.shape),
            ],
            out_specs=(
                whole((peers, feats, LO)),
                pl.BlockSpec((per, feats, LO), lambda i, rg: (i, 0, 0)),
            ),
            scratch_shapes=[
                pltpu.VMEM((eblocks * feats, LO), BF),
                pltpu.VMEM((peers, feats, LO), F32),
                pltpu.VMEM((per, feats, LO), F32),
            ],
        ),
        compiler_params=params(),
        name="backward",
    )(ranges, g_agg_t, src_t, trip, w_basis_t)


def weights_kernel(agg_t, g_pre, g_basis, trip, lines):
    feats, n_edges = agg_t.shape
    width = g_pre.shape[1]
    chunks, rows, _ = trip.shape
    steps = 4
    eb = n_edges // steps
    per = chunks // steps

    def body(a_ref, p_ref, g_ref, x_ref, out_ref, up, bt):
        i = pl.program_id(0)

        @pl.when(i == 0)
        def _():
            up[...] = jnp.zeros_like(up)
            bt[...] = jnp.zeros_like(bt)

        up[...] += nn(a_ref[...], p_ref[...])
        for a in range(per):
            top = g_ref[a].astype(BF)
            low = (g_ref[a] - top.astype(F32)).astype(BF)
            basis = x_ref[a].astype(BF)
            bt[...] += nt(basis, top) + nt(basis, low)

        @pl.when(i == steps - 1)
        def _():
            out_ref[:, :width] = up[...]
            tall = jnp.concatenate([bt[...], jnp.zeros((lines - rows, feats), F32)])
            out_ref[:, width:] = tall.T

    return pl.pallas_call(
        body,
        out_shape=jax.ShapeDtypeStruct((feats, width + lines), F32),
        grid=(steps,),
        in_specs=[
            pl.BlockSpec((feats, eb), lambda i: (0, i)),
            pl.BlockSpec((eb, width), lambda i: (i, 0)),
            pl.BlockSpec((per, feats, LO), lambda i: (i, 0, 0)),
            pl.BlockSpec((per, rows, LO), lambda i: (i, 0, 0)),
        ],
        out_specs=full((feats, width + lines)),
        scratch_shapes=[pltpu.VMEM((feats, width), F32), pltpu.VMEM((rows, feats), F32)],
        compiler_params=params(),
        name="weights",
    )(agg_t, g_pre, g_basis, trip)


def return_kernel(ret, send_idx, edges, piece):
    peers, feats, slot = ret.shape
    n_edges, width = edges.shape
    own = width // peers
    lines = own + piece.shape[1]
    per = 32
    steps = peers // per
    eblocks = n_edges // LO
    eb = 2048
    esteps = n_edges // eb

    def body(r_ref, i_ref, e_ref, p_ref, down_out, grad_out, acc, pm, oh, gacc):
        i = pl.program_id(0)

        @pl.when(i == 0)
        def _():
            acc[...] = jnp.zeros_like(acc)
            gacc[...] = jnp.zeros_like(gacc)

        @pl.when(i < steps)
        def _():
            for a in range(per):
                cols = slice(a * slot, (a + 1) * slot)
                lo, hi = split(i_ref[:, cols])
                rows = r_ref[i * per + a].astype(F32)
                for j in range(eblocks):
                    pm[j * feats:(j + 1) * feats, cols] = jnp.where(hi == j, rows, 0.0).astype(BF)
                oh[:, cols] = onehot(lo, slot)
            acc[...] += nt(pm[...], oh[...])

        @pl.when(i == steps - 1)
        def _():
            for j in range(eblocks):
                down_out[:, j * LO:(j + 1) * LO] = acc[j * feats:(j + 1) * feats].astype(BF)

        @pl.when(i >= steps)
        def _():
            k = i - steps
            gacc[...] += nn(down_out[:, pl.ds(pl.multiple_of(k * eb, eb), eb)], e_ref[...])

        @pl.when(i == steps + esteps - 1)
        def _():
            for q in range(width // feats):
                rows = gacc[:, q * feats:(q + 1) * feats].T.astype(BF)
                for k in range(feats // own):
                    grad_out[q * (feats // own) + k, :own] = rows[k * own:(k + 1) * own]
            grad_out[:, own:] = p_ref[...]

    return pl.pallas_call(
        body,
        out_shape=(
            jax.ShapeDtypeStruct((feats, n_edges), BF),
            jax.ShapeDtypeStruct((peers, lines, feats), BF),
        ),
        grid=(steps + esteps,),
        in_specs=[
            pl.BlockSpec(memory_space=pltpu.VMEM),
            pl.BlockSpec((1, per * slot), lambda i: (0, jnp.minimum(i, steps - 1))),
            pl.BlockSpec((eb, width), lambda i: (jnp.maximum(i - steps, 0), 0)),
            full(piece.shape),
        ],
        out_specs=(full((feats, n_edges)), full((peers, lines, feats))),
        scratch_shapes=[
            pltpu.VMEM((eblocks * feats, LO), F32),
            pltpu.VMEM((eblocks * feats, per * slot), BF),
            pltpu.VMEM((LO, per * slot), BF),
            pltpu.VMEM((feats, width), F32),
        ],
        compiler_params=params(),
        name="returned",
    )(ret, send_idx, edges, piece)


def edges_kernel(g_down_t, w_down_t):
    feats, n_edges = g_down_t.shape
    width = w_down_t.shape[1]
    eb = 1024

    def body(g_ref, w_ref, out_ref):
        out_ref[...] = tn(g_ref[...], w_ref[...]).astype(BF)

    return pl.pallas_call(
        body,
        out_shape=jax.ShapeDtypeStruct((n_edges, width), BF),
        grid=(n_edges // eb,),
        in_specs=[pl.BlockSpec((feats, eb), lambda i: (0, i)), full(w_down_t.shape)],
        out_specs=pl.BlockSpec((eb, width), lambda i: (i, 0)),
        compiler_params=params(),
        name="grad_edges",
    )(g_down_t, w_down_t)


def exchange(x, axes):
    return lax.all_to_all(x, axes, split_axis=0, concat_axis=0, tiled=True)


def graph_sum_kernel(got, n_dp):
    def body(x_ref, out_ref):
        mine = jnp.sum(x_ref[...].astype(F32), axis=0).astype(BF)
        out_ref[...] = jnp.broadcast_to(mine[None], out_ref.shape)

    return pl.pallas_call(
        body,
        out_shape=jax.ShapeDtypeStruct((n_dp,) + got.shape[1:], BF),
        compiler_params=params(),
        name="graph_sum",
    )(got)


def dp_sum_kernel(got, n_graph, own, cols):
    n_dp, lines, feats = got.shape

    def body(x_ref, out_ref):
        x = x_ref[...].astype(F32)
        down = jnp.sum(x[:, :own], axis=0)
        rest = x[:, own:].reshape(n_dp * (lines - own), feats).T
        mine = jnp.concatenate([down, rest[:cols]]).astype(BF)
        out_ref[...] = jnp.broadcast_to(mine[None], out_ref.shape)

    return pl.pallas_call(
        body,
        out_shape=jax.ShapeDtypeStruct((n_graph, own + cols, feats), BF),
        compiler_params=params(),
        name="dp_sum",
    )(got)


def scatter_dp(x, n_dp):
    d = lax.axis_index("dp")
    for bit in reversed(range(n_dp.bit_length() - 1)):
        half = x.shape[0] // 2
        b = (d >> bit) & 1
        keep = lax.dynamic_slice_in_dim(x, b * half, half, 0)
        give = lax.dynamic_slice_in_dim(x, (1 - b) * half, half, 0)
        x = keep + lax.ppermute(give, "dp", [(k, k ^ (1 << bit)) for k in range(n_dp)])
    return x


def share_out(part, width, peers):
    share, cols = part.shape
    part = part.astype(BF)
    views = [part[:, :width], part[:, width:]]
    views = [v.reshape(share, peers, -1).transpose(1, 0, 2) for v in views]
    wide = jnp.concatenate(views, axis=2)
    return jnp.pad(wide, ((0, 0), (0, 0), (0, -wide.shape[2] % 128)))


def make_shards(n_dp, n_graph):
    def shards(edges, send_rows, trip_src, trip_dst, basis_values, cotangent, w_down, w_up, w_basis):
        edge_rows = edges[0]
        basis = basis_values[0]
        n_edges, width = edge_rows.shape
        feats = w_down.shape[1]
        nb = basis.shape[0]
        sent = send_kernel(edge_rows, w_down, send_rows, n_graph)
        received = pltpu.with_memory_space_constraint(exchange(sent, "graph"), pltpu.VMEM)
        src, sent_now = lax.optimization_barrier((trip_src, sent))
        trip, ranges = sort_kernel(src, trip_dst, basis, n_graph)
        w_basis_t = jnp.pad(w_basis.T, ((0, 0), (0, trip.shape[1] - nb)))
        src_t, agg_t = forward_kernel(received, ranges, trip, w_basis_t, n_edges, nb)
        g_pre, g_agg_t = dense_kernel(agg_t, w_up, cotangent[0])
        g_received, g_basis = backward_kernel(
            g_agg_t, src_t, ranges, trip, w_basis_t, n_graph, nb
        )
        returned = exchange(g_received, "graph")
        n = n_dp * n_graph
        small = weights_kernel(agg_t, g_pre, g_basis, trip, n)
        part = scatter_dp(small, n_dp)
        returned, piece = lax.optimization_barrier((returned, share_out(part, width, n_graph)))
        returned = pltpu.with_memory_space_constraint(returned, pltpu.VMEM)
        g_down_t, slab = return_kernel(returned, send_rows, edge_rows, piece)
        own = width // n_graph
        cols = small.shape[1] // n_graph
        shared = exchange(graph_sum_kernel(exchange(slab, "graph"), n_dp), "dp")
        reduced = exchange(dp_sum_kernel(shared, n_graph, own, cols), "graph")
        grad_edges = edges_kernel(g_down_t, w_down.T)
        grad_down = reduced[:, :own].astype(F32).reshape(width, feats)
        grad_up = reduced[:, own:2 * own].astype(F32).reshape(width, feats).T
        grad_basis = reduced[:-(-nb // (cols - own)), 2 * own:].astype(F32).reshape(-1, feats)[:nb]
        return grad_edges[None], grad_down, grad_up, grad_basis

    return shards


def solution(mesh):
    shape = dict(mesh.shape)
    in_specs = (
        P("dp", "graph", None),
        P("dp", "graph"),
        P("dp", "graph"),
        P("dp", "graph"),
        P("dp", None, "graph"),
        P("dp", "graph", None),
        P(),
        P(),
        P(),
    )
    out_specs = (P("dp", "graph", None), P(), P(), P())
    return jax.shard_map(
        make_shards(shape["dp"], shape["graph"]),
        mesh=mesh,
        in_specs=in_specs,
        out_specs=out_specs,
        check_vma=False,
    )
```

```python
import jax
import jax.numpy as jnp
from jax import lax
from jax.experimental import pallas as pl
from jax.experimental.pallas import tpu as pltpu
from jax.sharding import PartitionSpec as P

LO = 256
BF = jnp.bfloat16
F32 = jnp.float32


def split(idx):
    return idx & (LO - 1), idx >> 8


def onehot(lo, width):
    rows = lax.broadcasted_iota(jnp.int32, (LO, width), 0)
    return jnp.where(rows == lo, 1.0, 0.0).astype(BF)


def nn(a, b):
    return jnp.dot(a, b, preferred_element_type=F32)


def nt(a, b):
    return lax.dot_general(a, b, (((1,), (1,)), ((), ())), preferred_element_type=F32)


def tn(a, b):
    return lax.dot_general(a, b, (((0,), (0,)), ((), ())), preferred_element_type=F32)


def pick(res, hi, blocks, feats, base=0):
    acc = jnp.zeros((feats, res.shape[1]), F32)
    for j in range(blocks):
        acc = jnp.where(hi == base + j, res[j * feats:(j + 1) * feats], acc)
    return acc


def params():
    return pltpu.CompilerParams(vmem_limit_bytes=48 * 1024 * 1024)


def full(shape):
    return pl.BlockSpec(shape, lambda i: (0,) * len(shape))


def send_kernel(edges, w_down, send_idx, peers):
    n_edges, width = edges.shape
    feats = w_down.shape[1]
    eb = 1024
    nd = n_edges // eb
    per = 16
    ng = peers // per
    slot = send_idx.shape[1] // peers
    blocks = n_edges // LO

    def body(e_ref, w_ref, i_ref, out_ref, table):
        i = pl.program_id(0)

        @pl.when(i < nd)
        def _():
            d = nn(e_ref[...], w_ref[...]).astype(BF).T
            for k in range(eb // LO):
                table[i * (eb // LO) + k] = d[:, k * LO:(k + 1) * LO]

        @pl.when(i >= nd)
        def _():
            tab = table[...].reshape(blocks * feats, LO)
            for a in range(per):
                lo, hi = split(i_ref[:, a * slot:(a + 1) * slot])
                res = nn(tab, onehot(lo, slot))
                out_ref[a] = pick(res, hi, blocks, feats).astype(BF)

    return pl.pallas_call(
        body,
        out_shape=jax.ShapeDtypeStruct((peers, feats, slot), BF),
        grid=(nd + ng,),
        in_specs=[
            pl.BlockSpec((eb, width), lambda i: (jnp.minimum(i, nd - 1), 0)),
            full(w_down.shape),
            pl.BlockSpec((1, per * slot), lambda i: (0, jnp.maximum(i - nd, 0))),
        ],
        out_specs=pl.BlockSpec((per, feats, slot), lambda i: (jnp.maximum(i - nd, 0), 0, 0)),
        scratch_shapes=[pltpu.VMEM((blocks, feats, LO), BF)],
        compiler_params=params(),
        name="send",
    )(edges, w_down, send_idx)


def sort_kernel(src, dst, basis, peers):
    trips = src.shape[1]
    nb = basis.shape[0]
    rows = -(-(nb + 4) // 16) * 16
    chunks = trips // LO
    tc = 1024
    steps = trips // tc

    def body(s_ref, d_ref, b_ref, x_out, range_out, oh_hi, first, pm, oh, acc):
        i = pl.program_id(0)

        @pl.when(i == 0)
        def _():
            acc[...] = jnp.zeros_like(acc)
            bucket = lax.broadcasted_iota(jnp.int32, (peers, trips), 0)
            hot = jnp.where(bucket == (s_ref[...] >> 8), 1.0, 0.0)
            oh_hi[...] = hot.astype(BF)
            total = jnp.broadcast_to(jnp.sum(hot, axis=1, keepdims=True), (peers, 128))
            high = jnp.floor(total * (1.0 / 256.0))
            low = total - high * 256.0
            r = lax.broadcasted_iota(jnp.int32, (peers, peers), 0)
            c = lax.broadcasted_iota(jnp.int32, (peers, peers), 1)
            before = jnp.where(c < r, 1.0, 0.0).astype(BF)
            start = 256.0 * nn(before, high.astype(BF)) + nn(before, low.astype(BF))
            first[...] = start
            edge = 256.0 * lax.broadcasted_iota(jnp.int32, (peers, 128), 1).astype(F32)
            b0 = jnp.sum(jnp.where(start + total <= edge, 1.0, 0.0), axis=0, keepdims=True)
            b1 = jnp.sum(jnp.where(start < edge + 256.0, 1.0, 0.0), axis=0, keepdims=True) - 1.0
            range_out[0:1] = jnp.minimum(b0, peers - 1.0).astype(jnp.int32)
            range_out[1:2] = b1.astype(jnp.int32)

        r = lax.broadcasted_iota(jnp.int32, (LO, LO), 0)
        c = lax.broadcasted_iota(jnp.int32, (LO, LO), 1)
        upto = jnp.where(r <= c, 1.0, 0.0).astype(BF)
        for a in range(tc // LO):
            cols = slice(a * LO, (a + 1) * LO)
            at = pl.multiple_of(i * tc + a * LO, LO)
            hot = oh_hi[:, pl.ds(at, LO)]
            count = nn(hot, upto)
            place = first[:, 0:1] + count - 1.0
            hot32 = hot.astype(F32)
            pos = jnp.sum(hot32 * place, axis=0, keepdims=True).astype(jnp.int32)
            first[...] += jnp.broadcast_to(count[:, LO - 1:LO], first.shape)
            s_lo, s_hi = split(s_ref[:, pl.ds(at, LO)])
            d_lo, d_hi = split(d_ref[:, cols])
            row = lax.broadcasted_iota(jnp.int32, (rows - nb, LO), 0)
            extra = jnp.where(row == 0, s_lo, jnp.where(row == 1, s_hi, jnp.where(row == 2, d_lo, jnp.where(row == 3, d_hi, 0))))
            x = jnp.concatenate([b_ref[:, cols].astype(F32), extra.astype(F32)], axis=0)
            lo, hi = split(pos)
            for j in range(chunks):
                pm[j * rows:(j + 1) * rows, cols] = jnp.where(hi == j, x, 0.0).astype(BF)
            oh[:, cols] = onehot(lo, LO)
        acc[...] += nt(pm[...], oh[...])

        @pl.when(i == steps - 1)
        def _():
            x_out[...] = acc[...].reshape(x_out.shape)

    return pl.pallas_call(
        body,
        out_shape=(
            jax.ShapeDtypeStruct((chunks, rows, LO), F32),
            jax.ShapeDtypeStruct((2, 128), jnp.int32),
        ),
        grid=(steps,),
        in_specs=[
            full(src.shape),
            pl.BlockSpec((1, tc), lambda i: (0, i)),
            pl.BlockSpec((nb, tc), lambda i: (0, i)),
        ],
        out_specs=(full((chunks, rows, LO)), full((2, 128))),
        scratch_shapes=[
            pltpu.VMEM((peers, trips), BF),
            pltpu.VMEM((peers, 128), F32),
            pltpu.VMEM((chunks * rows, tc), BF),
            pltpu.VMEM((LO, tc), BF),
            pltpu.VMEM((chunks * rows, LO), F32),
        ],
        compiler_params=params(),
        name="order",
    )(src, dst, basis)


NEAR = 3


def forward_kernel(recv, ranges, trip, w_basis_t, n_edges, nb):
    peers, feats, _ = recv.shape
    chunks, rows, _ = trip.shape
    per = 16
    steps = chunks // per
    eblocks = n_edges // LO

    def body(rg, r_ref, x_ref, w_ref, src_out, agg_out, acc, pm, oh, source):
        i = pl.program_id(0)

        @pl.when(i == 0)
        def _():
            acc[...] = jnp.zeros_like(acc)

        def ids(a, k):
            return x_ref[a, nb + k:nb + k + 1].astype(jnp.int32)

        far = jnp.int32(0)
        for a in range(per):
            b0 = rg[0, i * per + a]
            far = jnp.maximum(far, rg[1, i * per + a] - b0)
            hot = onehot(ids(a, 0), LO)
            hi = ids(a, 1)
            at = jnp.minimum(b0, peers - NEAR)
            near = r_ref[pl.ds(at, NEAR)].reshape(NEAR * feats, LO)
            source[a] = pick(nn(near, hot), hi, NEAR, feats, at)

        @pl.when(far >= NEAR)
        def _():
            for a in range(per):
                def more(b, _, a=a):
                    res = nn(r_ref[b], onehot(ids(a, 0), LO))
                    source[a] = jnp.where(ids(a, 1) == b, res, source[a])
                    return 0
                lax.fori_loop(rg[0, i * per + a] + NEAR, rg[1, i * per + a] + 1, more, 0)

        for a in range(per):
            cols = slice(a * LO, (a + 1) * LO)
            src_out[a] = source[a].astype(BF)
            product = source[a] * nn(w_ref[...], x_ref[a].astype(BF))
            hi = ids(a, 3)
            for j in range(eblocks):
                pm[j * feats:(j + 1) * feats, cols] = jnp.where(hi == j, product, 0.0).astype(BF)
            oh[:, cols] = onehot(ids(a, 2), LO)
        acc[...] += nt(pm[...], oh[...])

        @pl.when(i == steps - 1)
        def _():
            for j in range(eblocks):
                agg_out[:, j * LO:(j + 1) * LO] = acc[j * feats:(j + 1) * feats].astype(BF)

    def whole(shape):
        return pl.BlockSpec(shape, lambda i, rg: (0,) * len(shape))

    return pl.pallas_call(
        body,
        out_shape=(
            jax.ShapeDtypeStruct((chunks, feats, LO), BF),
            jax.ShapeDtypeStruct((feats, n_edges), BF),
        ),
        grid_spec=pltpu.PrefetchScalarGridSpec(
            num_scalar_prefetch=1,
            grid=(steps,),
            in_specs=[
                pl.BlockSpec(memory_space=pltpu.VMEM),
                pl.BlockSpec((per, rows, LO), lambda i, rg: (i, 0, 0)),
                whole(w_basis_t.shape),
            ],
            out_specs=(
                pl.BlockSpec((per, feats, LO), lambda i, rg: (i, 0, 0)),
                whole((feats, n_edges)),
            ),
            scratch_shapes=[
                pltpu.VMEM((eblocks * feats, LO), F32),
                pltpu.VMEM((eblocks * feats, per * LO), BF),
                pltpu.VMEM((LO, per * LO), BF),
                pltpu.VMEM((per, feats, LO), F32),
            ],
        ),
        compiler_params=params(),
        name="forward",
    )(ranges, recv, trip, w_basis_t)


def dense_kernel(agg_t, w_up, cot):
    feats, n_edges = agg_t.shape
    width = w_up.shape[1]
    eb = 1024
    steps = n_edges // eb

    def body(a_ref, w_ref, c_ref, p_out, g_out):
        for k in range(eb // 256):
            r = slice(k * 256, (k + 1) * 256)
            pre = tn(a_ref[:, r], w_ref[...])
            t = 0.5 * jnp.tanh(0.5 * pre)
            g_pre = (c_ref[r].astype(F32) * (0.5 + t) * (1.0 + pre * (0.5 - t))).astype(BF)
            p_out[r] = g_pre
            g_out[:, r] = nt(w_ref[...], g_pre).astype(BF)

    return pl.pallas_call(
        body,
        out_shape=(
            jax.ShapeDtypeStruct((n_edges, width), BF),
            jax.ShapeDtypeStruct((feats, n_edges), BF),
        ),
        grid=(steps,),
        in_specs=[
            pl.BlockSpec((feats, eb), lambda i: (0, i)),
            full(w_up.shape),
            pl.BlockSpec((eb, width), lambda i: (i, 0)),
        ],
        out_specs=(
            pl.BlockSpec((eb, width), lambda i: (i, 0)),
            pl.BlockSpec((feats, eb), lambda i: (0, i)),
        ),
        compiler_params=params(),
        name="dense",
    )(agg_t, w_up, cot)


def backward_kernel(g_agg_t, src_t, ranges, trip, w_basis_t, peers, nb):
    feats, n_edges = g_agg_t.shape
    chunks, rows, _ = trip.shape
    per = 8
    steps = chunks // per
    eblocks = n_edges // LO

    def body(rg, g_ref, st_ref, x_ref, w_ref, out_ref, gb_out, table, acc, source):
        i = pl.program_id(0)

        @pl.when(i == 0)
        def _():
            acc[...] = jnp.zeros_like(acc)
            for j in range(eblocks):
                table[j * feats:(j + 1) * feats] = g_ref[:, j * LO:(j + 1) * LO]

        def ids(a, k):
            return x_ref[a, nb + k:nb + k + 1].astype(jnp.int32)

        far = jnp.int32(0)
        for a in range(per):
            g_trip = pick(nn(table[...], onehot(ids(a, 2), LO)), ids(a, 3), eblocks, feats)
            gb_out[a] = g_trip * st_ref[a].astype(F32)
            source[a] = g_trip * nn(w_ref[...], x_ref[a].astype(BF))
        for a in range(per):
            b0 = rg[0, i * per + a]
            far = jnp.maximum(far, rg[1, i * per + a] - b0)
            hot = onehot(ids(a, 0), LO)
            hi = ids(a, 1)
            at = jnp.minimum(b0, peers - NEAR)
            near = jnp.concatenate([jnp.where(hi == at + n, source[a], 0.0) for n in range(NEAR)]).astype(BF)
            acc[pl.ds(at, NEAR)] += nt(near, hot).reshape(NEAR, feats, LO)

        @pl.when(far >= NEAR)
        def _():
            for a in range(per):
                def more(b, _, a=a):
                    part = jnp.where(ids(a, 1) == b, source[a], 0.0).astype(BF)
                    acc[b] += nt(part, onehot(ids(a, 0), LO))
                    return 0
                lax.fori_loop(rg[0, i * per + a] + NEAR, rg[1, i * per + a] + 1, more, 0)

        @pl.when(i == steps - 1)
        def _():
            out_ref[...] = acc[...].astype(BF)

    def whole(shape):
        return pl.BlockSpec(shape, lambda i, rg: (0,) * len(shape))

    return pl.pallas_call(
        body,
        out_shape=(
            jax.ShapeDtypeStruct((peers, feats, LO), BF),
            jax.ShapeDtypeStruct((chunks, feats, LO), F32),
        ),
        grid_spec=pltpu.PrefetchScalarGridSpec(
            num_scalar_prefetch=1,
            grid=(steps,),
            in_specs=[
                whole(g_agg_t.shape),
                pl.BlockSpec((per, feats, LO), lambda i, rg: (i, 0, 0)),
                pl.BlockSpec((per, rows, LO), lambda i, rg: (i, 0, 0)),
                whole(w_basis_t.shape),
            ],
            out_specs=(
                whole((peers, feats, LO)),
                pl.BlockSpec((per, feats, LO), lambda i, rg: (i, 0, 0)),
            ),
            scratch_shapes=[
                pltpu.VMEM((eblocks * feats, LO), BF),
                pltpu.VMEM((peers, feats, LO), F32),
                pltpu.VMEM((per, feats, LO), F32),
            ],
        ),
        compiler_params=params(),
        name="backward",
    )(ranges, g_agg_t, src_t, trip, w_basis_t)


def weights_kernel(agg_t, g_pre, g_basis, trip, lines):
    feats, n_edges = agg_t.shape
    width = g_pre.shape[1]
    chunks, rows, _ = trip.shape
    steps = 4
    eb = n_edges // steps
    per = chunks // steps

    def body(a_ref, p_ref, g_ref, x_ref, out_ref, up, bt):
        i = pl.program_id(0)

        @pl.when(i == 0)
        def _():
            up[...] = jnp.zeros_like(up)
            bt[...] = jnp.zeros_like(bt)

        up[...] += nn(a_ref[...], p_ref[...])
        for a in range(per):
            top = g_ref[a].astype(BF)
            low = (g_ref[a] - top.astype(F32)).astype(BF)
            basis = x_ref[a].astype(BF)
            bt[...] += nt(basis, top) + nt(basis, low)

        @pl.when(i == steps - 1)
        def _():
            out_ref[:, :width] = up[...]
            tall = jnp.concatenate([bt[...], jnp.zeros((lines - rows, feats), F32)])
            out_ref[:, width:] = tall.T

    return pl.pallas_call(
        body,
        out_shape=jax.ShapeDtypeStruct((feats, width + lines), F32),
        grid=(steps,),
        in_specs=[
            pl.BlockSpec((feats, eb), lambda i: (0, i)),
            pl.BlockSpec((eb, width), lambda i: (i, 0)),
            pl.BlockSpec((per, feats, LO), lambda i: (i, 0, 0)),
            pl.BlockSpec((per, rows, LO), lambda i: (i, 0, 0)),
        ],
        out_specs=full((feats, width + lines)),
        scratch_shapes=[pltpu.VMEM((feats, width), F32), pltpu.VMEM((rows, feats), F32)],
        compiler_params=params(),
        name="weights",
    )(agg_t, g_pre, g_basis, trip)


def return_kernel(ret, send_idx, edges, piece):
    peers, feats, slot = ret.shape
    n_edges, width = edges.shape
    own = width // peers
    lines = own + piece.shape[1]
    per = 32
    steps = peers // per
    eblocks = n_edges // LO
    eb = 2048
    esteps = n_edges // eb

    def body(r_ref, i_ref, e_ref, p_ref, down_out, grad_out, acc, pm, oh, gacc):
        i = pl.program_id(0)

        @pl.when(i == 0)
        def _():
            acc[...] = jnp.zeros_like(acc)
            gacc[...] = jnp.zeros_like(gacc)

        @pl.when(i < steps)
        def _():
            for a in range(per):
                cols = slice(a * slot, (a + 1) * slot)
                lo, hi = split(i_ref[:, cols])
                rows = r_ref[i * per + a].astype(F32)
                for j in range(eblocks):
                    pm[j * feats:(j + 1) * feats, cols] = jnp.where(hi == j, rows, 0.0).astype(BF)
                oh[:, cols] = onehot(lo, slot)
            acc[...] += nt(pm[...], oh[...])

        @pl.when(i == steps - 1)
        def _():
            for j in range(eblocks):
                down_out[:, j * LO:(j + 1) * LO] = acc[j * feats:(j + 1) * feats].astype(BF)

        @pl.when(i >= steps)
        def _():
            k = i - steps
            gacc[...] += nn(down_out[:, pl.ds(pl.multiple_of(k * eb, eb), eb)], e_ref[...])

        @pl.when(i == steps + esteps - 1)
        def _():
            for q in range(width // feats):
                rows = gacc[:, q * feats:(q + 1) * feats].T.astype(BF)
                for k in range(feats // own):
                    grad_out[q * (feats // own) + k, :own] = rows[k * own:(k + 1) * own]
            grad_out[:, own:] = p_ref[...]

    return pl.pallas_call(
        body,
        out_shape=(
            jax.ShapeDtypeStruct((feats, n_edges), BF),
            jax.ShapeDtypeStruct((peers, lines, feats), BF),
        ),
        grid=(steps + esteps,),
        in_specs=[
            pl.BlockSpec(memory_space=pltpu.VMEM),
            pl.BlockSpec((1, per * slot), lambda i: (0, jnp.minimum(i, steps - 1))),
            pl.BlockSpec((eb, width), lambda i: (jnp.maximum(i - steps, 0), 0)),
            full(piece.shape),
        ],
        out_specs=(full((feats, n_edges)), full((peers, lines, feats))),
        scratch_shapes=[
            pltpu.VMEM((eblocks * feats, LO), F32),
            pltpu.VMEM((eblocks * feats, per * slot), BF),
            pltpu.VMEM((LO, per * slot), BF),
            pltpu.VMEM((feats, width), F32),
        ],
        compiler_params=params(),
        name="returned",
    )(ret, send_idx, edges, piece)


def edges_kernel(g_down_t, w_down_t):
    feats, n_edges = g_down_t.shape
    width = w_down_t.shape[1]
    eb = 1024

    def body(g_ref, w_ref, out_ref):
        out_ref[...] = tn(g_ref[...], w_ref[...]).astype(BF)

    return pl.pallas_call(
        body,
        out_shape=jax.ShapeDtypeStruct((n_edges, width), BF),
        grid=(n_edges // eb,),
        in_specs=[pl.BlockSpec((feats, eb), lambda i: (0, i)), full(w_down_t.shape)],
        out_specs=pl.BlockSpec((eb, width), lambda i: (i, 0)),
        compiler_params=params(),
        name="grad_edges",
    )(g_down_t, w_down_t)


def exchange(x, axes):
    return lax.all_to_all(x, axes, split_axis=0, concat_axis=0, tiled=True)


def graph_sum_kernel(got, n_dp):
    def body(x_ref, out_ref):
        mine = jnp.sum(x_ref[...].astype(F32), axis=0).astype(BF)
        out_ref[...] = jnp.broadcast_to(mine[None], out_ref.shape)

    return pl.pallas_call(
        body,
        out_shape=jax.ShapeDtypeStruct((n_dp,) + got.shape[1:], BF),
        compiler_params=params(),
        name="graph_sum",
    )(got)


def dp_sum_kernel(got, n_graph, own, cols):
    n_dp, lines, feats = got.shape

    def body(x_ref, out_ref):
        x = x_ref[...].astype(F32)
        down = jnp.sum(x[:, :own], axis=0)
        rest = x[:, own:].reshape(n_dp * (lines - own), feats).T
        mine = jnp.concatenate([down, rest[:cols]]).astype(BF)
        out_ref[...] = jnp.broadcast_to(mine[None], out_ref.shape)

    return pl.pallas_call(
        body,
        out_shape=jax.ShapeDtypeStruct((n_graph, own + cols, feats), BF),
        compiler_params=params(),
        name="dp_sum",
    )(got)


def scatter_dp(x, n_dp):
    d = lax.axis_index("dp")
    for bit in reversed(range(n_dp.bit_length() - 1)):
        half = x.shape[0] // 2
        b = (d >> bit) & 1
        keep = lax.dynamic_slice_in_dim(x, b * half, half, 0)
        give = lax.dynamic_slice_in_dim(x, (1 - b) * half, half, 0)
        x = keep + lax.ppermute(give, "dp", [(k, k ^ (1 << bit)) for k in range(n_dp)])
    return x


def share_out(part, width, peers):
    share, cols = part.shape
    part = part.astype(BF)
    views = [part[:, :width], part[:, width:]]
    views = [v.reshape(share, peers, -1).transpose(1, 0, 2) for v in views]
    wide = jnp.concatenate(views, axis=2)
    return jnp.pad(wide, ((0, 0), (0, 0), (0, -wide.shape[2] % 128)))


def make_shards(n_dp, n_graph):
    def shards(edges, send_rows, trip_src, trip_dst, basis_values, cotangent, w_down, w_up, w_basis):
        edge_rows = edges[0]
        basis = basis_values[0]
        n_edges, width = edge_rows.shape
        feats = w_down.shape[1]
        nb = basis.shape[0]
        sent = send_kernel(edge_rows, w_down, send_rows, n_graph)
        received = pltpu.with_memory_space_constraint(exchange(sent, "graph"), pltpu.VMEM)
        src, sent_now = lax.optimization_barrier((trip_src, sent))
        trip, ranges = sort_kernel(src, trip_dst, basis, n_graph)
        w_basis_t = jnp.pad(w_basis.T, ((0, 0), (0, trip.shape[1] - nb)))
        src_t, agg_t = forward_kernel(received, ranges, trip, w_basis_t, n_edges, nb)
        g_pre, g_agg_t = dense_kernel(agg_t, w_up, cotangent[0])
        g_received, g_basis = backward_kernel(
            g_agg_t, src_t, ranges, trip, w_basis_t, n_graph, nb
        )
        returned = exchange(g_received, "graph")
        n = n_dp * n_graph
        small = weights_kernel(agg_t, g_pre, g_basis, trip, n)
        part = scatter_dp(small, n_dp)
        returned, piece = lax.optimization_barrier((returned, share_out(part, width, n_graph)))
        returned = pltpu.with_memory_space_constraint(returned, pltpu.VMEM)
        g_down_t, slab = return_kernel(returned, send_rows, edge_rows, piece)
        own = width // n_graph
        cols = small.shape[1] // n_graph
        shared = exchange(graph_sum_kernel(exchange(slab, "graph"), n_dp), "dp")
        reduced = exchange(dp_sum_kernel(shared, n_graph, own, cols), "graph")
        grad_edges = edges_kernel(g_down_t, w_down.T)
        grad_down = reduced[:, :own].astype(F32).reshape(width, feats)
        grad_up = reduced[:, own:2 * own].astype(F32).reshape(width, feats).T
        grad_basis = reduced[:-(-nb // (cols - own)), 2 * own:].astype(F32).reshape(-1, feats)[:nb]
        return grad_edges[None], grad_down, grad_up, grad_basis

    return shards


def solution(mesh):
    shape = dict(mesh.shape)
    in_specs = (
        P("dp", "graph", None),
        P("dp", "graph"),
        P("dp", "graph"),
        P("dp", "graph"),
        P("dp", None, "graph"),
        P("dp", "graph", None),
        P(),
        P(),
        P(),
    )
    out_specs = (P("dp", "graph", None), P(), P(), P())
    return jax.shard_map(
        make_shards(shape["dp"], shape["graph"]),
        mesh=mesh,
        in_specs=in_specs,
        out_specs=out_specs,
        check_vma=False,
    )
```
